32 devices in a mesh: pix: 8 (over z, y), rep: 4 (over x, core).
Axes of the slice: x: 2, y: 2, z: 4, core: 2. Of those that a mesh axis runs over, the one named last changes fastest.
Arguments:
- sky_cube: float32 [4, 512, 65536], P('rep', None, 'pix'), may hold values from -6 to 10
- pixel_mask: int32 [4, 65536], P('rep', 'pix'), may hold values 0 or 1
- noise_cov: float32 [512, 512], replicated, may hold values from -1 to 2, as said below
Outputs:
- power_cube: float32 [4, 512, 65536], P('rep', 'pix')
The draws below stay inside these ranges and needn't reach their ends.
Inputs may be any that keep to these rules, and one draw needn't show every extreme that they name: `noise_cov`: symmetric; each diagonal entry exceeds the sum of magnitudes off the diagonal in its row.
All inputs are finite; a program needn't handle non-finite values. No bound on the sum of `pixel_mask` on one device may be relied on, other than what follows from the above.
Results may differ from the reference program's by a relative error of at most 0.00012.
Values sent between devices are 32-bit elements; how exact they have to be, the bound alone decides.
A program may use at most 320 MiB of HBM per device.

```python
import math
import jax
import jax.numpy as jnp
from jax import lax

F = 512
SY = 256
SX = 256
PIX = 65536
PATCHES = 4


def draw_sky_cube(key, part):
    keys = jax.random.split(key, 5)
    shape_pix = (PATCHES, 1, PIX)
    chan = (1.0 + jnp.arange(F, dtype=jnp.float32) / F)[None, :, None]
    amp_sync = jnp.exp(jax.random.uniform(keys[0], shape_pix, jnp.float32, math.log(0.5), math.log(3.0)))
    beta_sync = jax.random.uniform(keys[1], shape_pix, jnp.float32, 2.5, 3.1)
    amp_free = jnp.exp(jax.random.uniform(keys[2], shape_pix, jnp.float32, math.log(0.2), math.log(1.0)))
    beta_free = jax.random.uniform(keys[3], shape_pix, jnp.float32, 2.0, 2.2)
    noise = jax.random.truncated_normal(keys[4], -6.0, 6.0, (PATCHES, F, PIX), jnp.float32)
    fore = amp_sync * jnp.exp(-beta_sync * jnp.log(chan)) + amp_free * jnp.exp(-beta_free * jnp.log(chan))
    return (fore + noise).astype(jnp.float32)


def draw_noise_cov(key, part):
    keys = jax.random.split(key, 2)
    diag_vals = jnp.exp(jax.random.uniform(keys[0], (F,), jnp.float32, 0.0, math.log(2.0)))
    off = jax.random.uniform(keys[1], (F, F), jnp.float32, -0.9 / F, 0.9 / F)
    off = (off + off.T) * 0.5
    idx = jnp.arange(F, dtype=jnp.int32)
    ident = (idx[:, None] == idx[None, :]).astype(jnp.float32)
    return (off * (1.0 - ident) + ident * diag_vals[None, :]).astype(jnp.float32)


def with_ends(values, stream_key, smallest, top_value):
    spot = [jax.random.randint(jax.random.fold_in(stream_key, axis), (), 0, length) for axis, length in enumerate(values.shape)]
    widest = values.shape.index(max(values.shape))
    beside = spot[:widest] + [(spot[widest] + 1) % values.shape[widest]] + spot[widest + 1:]
    return values.at[tuple(spot)].set(smallest).at[tuple(beside)].set(top_value)


def setup_inputs(seed: int = 0) -> dict:
    seeds = jax.random.split(jax.random.key(seed), 4)
    return {
        "sky_cube": draw_sky_cube(jax.random.fold_in(seeds[3], 71), 0),
        "pixel_mask": with_ends((jax.random.randint(seeds[1], (PATCHES, PIX), 0, 10) < 9).astype(jnp.int32), jax.random.fold_in(seeds[1], 1), 0, 1),
        "noise_cov": draw_noise_cov(jax.random.fold_in(seeds[3], 71), 0),
    }


HI = lax.Precision.HIGHEST

def dft_pair(length):
    idx = jnp.arange(length, dtype=jnp.int32)
    phase = (idx[:, None] * idx[None, :] % length).astype(jnp.float32) * (2.0 * math.pi / length)
    return (jnp.cos(phase), jnp.sin(phase))

def los_table(length):
    idx = jnp.arange(length, dtype=jnp.int32)
    half_len = length // 2
    freq = jnp.where(idx <= half_len, idx, idx - half_len)
    phase = (freq[:, None] * idx[None, :] % length).astype(jnp.float32) * (2.0 * math.pi / length)
    values = jnp.where((idx <= half_len)[:, None], jnp.cos(phase), jnp.sin(phase))
    edge = jnp.logical_or(idx == 0, idx == half_len)
    scale = jnp.where(edge, math.sqrt(1.0 / length), math.sqrt(2.0 / length)).astype(jnp.float32)
    return values * scale[:, None]

def sky_power(planes, rows_y, cols_x):
    count = planes.shape[0]
    field = planes.reshape(count, rows_y, cols_x)
    cos_x, sin_x = dft_pair(cols_x)
    cos_y, sin_y = dft_pair(rows_y)
    both_x = jnp.concatenate([cos_x, sin_x], axis=1)
    both_y = jnp.concatenate([cos_y, sin_y], axis=0)
    first = jnp.einsum('kyx,xw->kyw', field, both_x, precision=HI)
    second = jnp.einsum('vy,kyw->kvw', both_y, first, precision=HI)
    real_part = second[:, :rows_y, :cols_x] - second[:, rows_y:, cols_x:]
    imag_part = -(second[:, rows_y:, :cols_x] + second[:, :rows_y, cols_x:])
    power_map = (real_part * real_part + imag_part * imag_part) / float(rows_y * cols_x)
    return power_map.reshape(count, rows_y * cols_x)

def reference(sky_cube, pixel_mask, noise_cov):
    live = pixel_mask.astype(jnp.float32)[:, None, :]
    masked = sky_cube * live

    def patch_cov(patch):
        return jnp.dot(patch, patch.T, precision=HI)
    data_cov = lax.optimization_barrier(jnp.sum(lax.map(patch_cov, masked), axis=0))
    regular = data_cov / float(PATCHES * PIX) + noise_cov
    factor = jnp.linalg.cholesky(regular)
    filter_t = jax.scipy.linalg.cho_solve((factor, True), noise_cov)
    table = los_table(F)

    def patch_power(patch):
        cleaned = jnp.dot(filter_t.T, patch, precision=HI)
        spectra = jnp.dot(table, cleaned, precision=HI)
        groups = spectra.reshape(F // 8, 8, PIX)
        result = lax.map(lambda planes: sky_power(planes, SY, SX), groups)
        return result.reshape(F, PIX)
    return lax.map(patch_power, masked)
```

```python
import functools
import math

import jax
import jax.numpy as jnp
import ml_dtypes
import numpy as np
from jax import lax
from jax.experimental import pallas as pl
from jax.experimental.pallas import tpu as pltpu
from jax.sharding import PartitionSpec as P

F = 512
SY = 256
SX = 256
BLOCK = 128
GROUP = 8
LANES = 128
VMEM_LIMIT = 60 * 1024 * 1024

HI = lax.Precision.HIGHEST
MID = lax.Precision.HIGH
MESH = pl.DeviceIdType.MESH


def dft_pair(length):
    idx = jnp.arange(length, dtype=jnp.int32)
    phase = (idx[:, None] * idx[None, :] % length).astype(jnp.float32) * (2.0 * math.pi / length)
    return (jnp.cos(phase), jnp.sin(phase))


def los_table(length):
    idx = np.arange(length)
    half_len = length // 2
    freq = np.where(idx <= half_len, idx, idx - half_len)
    phase = (freq[:, None] * idx[None, :] % length) * (2.0 * math.pi / length)
    values = np.where((idx <= half_len)[:, None], np.cos(phase), np.sin(phase))
    edge = np.logical_or(idx == 0, idx == half_len)
    scale = np.where(edge, math.sqrt(1.0 / length), math.sqrt(2.0 / length))
    return (values * scale[:, None]).astype(np.float32)


def sky_power(planes, rows_y, cols_x):
    count = planes.shape[0]
    field = planes.reshape(count, rows_y, cols_x)
    cos_x, sin_x = dft_pair(cols_x)
    cos_y, sin_y = dft_pair(rows_y)
    both_x = jnp.concatenate([cos_x, sin_x], axis=1)
    both_y = jnp.concatenate([cos_y, sin_y], axis=0)
    first = jnp.einsum("kyx,xw->kyw", field, both_x, precision=MID)
    second = jnp.einsum("vy,kyw->kvw", both_y, first, precision=MID)
    real_part = second[:, :rows_y, :cols_x] - second[:, rows_y:, cols_x:]
    imag_part = -(second[:, rows_y:, :cols_x] + second[:, :rows_y, cols_x:])
    power_map = (real_part * real_part + imag_part * imag_part) / float(rows_y * cols_x)
    return power_map.reshape(count, rows_y * cols_x)


def sum_kernel(axes, x_ref, o_ref, acc, full, got, send_sem, recv_sem):
    where = {name: lax.axis_index(name) for name, _ in axes}
    steps = []
    for name, size in axes:
        bit = 1
        while bit < size:
            steps.append((name, bit))
            bit *= 2

    def partner(name, bit):
        me = where[name]
        mine = lax.rem(me // bit, 2)
        return mine, {name: me + bit * (1 - 2 * mine)}

    barrier = pltpu.get_barrier_semaphore()
    for name, bit in steps:
        _, other = partner(name, bit)
        pl.semaphore_signal(barrier, inc=1, device_id=other, device_id_type=MESH)
    pl.semaphore_wait(barrier, len(steps))

    total = x_ref.shape[0]
    rows, start, offset = total, 0, 0
    acc[...] = x_ref[...]
    plan = []
    for n, (name, bit) in enumerate(steps):
        mine, other = partner(name, bit)
        split = rows % 16 == 0
        if split:
            rows //= 2
            away = start + (1 - mine) * rows
            start = start + mine * rows
        else:
            away = start
        plan.append((other, split, start, rows, mine))
        if split:
            away = pl.multiple_of(away, 8)
        here = pl.multiple_of(start, 8)
        source = x_ref if n == 0 else acc
        copy = pltpu.make_async_remote_copy(
            src_ref=source.at[pl.ds(away, rows)],
            dst_ref=got.at[pl.ds(offset, rows)],
            send_sem=send_sem.at[n],
            recv_sem=recv_sem.at[n],
            device_id=other,
            device_id_type=MESH,
        )
        copy.start()
        copy.wait()
        acc[pl.ds(here, rows)] = acc[pl.ds(here, rows)] + got[pl.ds(offset, rows)]
        offset += rows
    last = pl.ds(pl.multiple_of(start, 8), rows)
    full[last] = acc[last]
    for n in reversed(range(len(steps))):
        other, split, start, rows, mine = plan[n]
        if not split:
            continue
        here = pl.multiple_of(start, 8)
        copy = pltpu.make_async_remote_copy(
            src_ref=full.at[pl.ds(here, rows)],
            dst_ref=full.at[pl.ds(here, rows)],
            send_sem=send_sem.at[len(steps) + n],
            recv_sem=recv_sem.at[len(steps) + n],
            device_id=other,
            device_id_type=MESH,
        )
        copy.start()
        copy.wait()
    o_ref[...] = full[...]


def reduce_cov(partial_value, sizes):
    axes = [("rep", sizes["rep"]), ("pix", sizes["pix"])]
    rows, depth, count = partial_value.shape[0], 0, 0
    for _, size in axes:
        for _ in range(size.bit_length() - 1):
            if rows % 16 == 0:
                rows //= 2
            depth += rows
            count += 1
    vmem = pl.BlockSpec(memory_space=pltpu.VMEM)
    return pl.pallas_call(
        functools.partial(sum_kernel, axes),
        out_shape=jax.ShapeDtypeStruct(partial_value.shape, jnp.float32),
        in_specs=[vmem],
        out_specs=vmem,
        scratch_shapes=[
            pltpu.VMEM(partial_value.shape, jnp.float32),
            pltpu.VMEM(partial_value.shape, jnp.float32),
            pltpu.VMEM((depth, partial_value.shape[1]), jnp.float32),
            pltpu.SemaphoreType.DMA((2 * count,)),
            pltpu.SemaphoreType.DMA((2 * count,)),
        ],
        compiler_params=pltpu.CompilerParams(collective_id=0, has_side_effects=True),
        name="cov_sum",
    )(partial_value)


def block_inverse(a):
    size = a.shape[0]
    row_id = lax.broadcasted_iota(jnp.int32, (size, size), 0)
    col_id = lax.broadcasted_iota(jnp.int32, (size, size), 1)
    for j in range(size):
        pivot = 1.0 / a[j : j + 1, j : j + 1]
        row = a[j : j + 1, :] * pivot
        col = a[:, j : j + 1]
        base = jnp.where(col_id == j, 0.0, a)
        row = jnp.where(col_id[:1] == j, pivot, row)
        a = jnp.where(row_id == j, row, base - col * row)
    return a


def solve_kernel(scale, cov_ref, noise_ref, table_ref, o_ref, a_ref):
    size = cov_ref.shape[0]
    a_ref[...] = cov_ref[...] * scale + noise_ref[...]
    o_ref[...] = lax.dot_general(
        noise_ref[...],
        table_ref[...],
        (((1,), (1,)), ((), ())),
        precision=HI,
        preferred_element_type=jnp.float32,
    )
    blocks = size // BLOCK

    def mul(x, y):
        return jnp.dot(x, y, precision=HI, preferred_element_type=jnp.float32)

    def step(k, _):
        here = pl.ds(pl.multiple_of(k * BLOCK, BLOCK), BLOCK)
        inverse = block_inverse(a_ref[here, here])
        panel = mul(inverse, a_ref[here, :])
        right = mul(inverse, o_ref[here, :])
        for i in range(blocks):
            rows = pl.ds(i * BLOCK, BLOCK)

            @pl.when(k != i)
            def _():
                factor = a_ref[rows, here]
                o_ref[rows, :] = o_ref[rows, :] - mul(factor, right)

                @pl.when(k < blocks - 1)
                def _():
                    a_ref[rows, :] = a_ref[rows, :] - mul(factor, panel)

        o_ref[here, :] = right
        a_ref[here, :] = panel
        return 0

    lax.fori_loop(0, blocks, step, 0)


def folded_transpose(data_cov, scale, noise_cov, table):
    vmem = pl.BlockSpec(memory_space=pltpu.VMEM)
    return pl.pallas_call(
        functools.partial(solve_kernel, scale),
        out_shape=jax.ShapeDtypeStruct(data_cov.shape, jnp.float32),
        in_specs=[vmem] * 3,
        out_specs=vmem,
        scratch_shapes=[pltpu.VMEM(data_cov.shape, jnp.float32)],
        name="filter_solve",
    )(data_cov, noise_cov, table)

def split(x):
    high = x.astype(jnp.bfloat16)
    return high, (x - high.astype(jnp.float32)).astype(jnp.bfloat16)


def dot3(left, right):
    (lh, ll), (rh, rl) = left, right
    one = functools.partial(jnp.dot, preferred_element_type=jnp.float32)
    return one(lh, rh) + (one(lh, rl) + one(ll, rh))


def split_table(values):
    high = values.astype(ml_dtypes.bfloat16)
    low = (values - high.astype(np.float64)).astype(ml_dtypes.bfloat16)
    return jnp.asarray(high), jnp.asarray(low)


def packed_x(length):
    idx = np.arange(length)
    half = length // 2
    phase = lambda freq: (idx[:, None] * freq[None, :] % length) * (2.0 * math.pi / length)
    cosines = np.cos(phase(np.arange(half + 1)))
    sines = np.sin(phase(np.arange(1, half)))
    return np.concatenate([cosines, sines], axis=1)


def full_y(length):
    idx = np.arange(length)
    phase = (idx[:, None] * idx[None, :] % length) * (2.0 * math.pi / length)
    return np.concatenate([np.cos(phase), np.sin(phase)], axis=0)


def spread_kernel(
    n, sky_ref, mask_ref, mix_ref, dxh_ref, dxl_ref, z_ref,
    sky, high, low, out, load_sem, send_sem, recv_sem, own_sem,
):
    me = lax.axis_index("pix")
    rows = sky.shape[0]
    width = sky.shape[2]
    chunks = out.shape[0]
    group = math.gcd(rows, GROUP)
    step = n * 8
    tall = 8 * width // LANES

    barrier = pltpu.get_barrier_semaphore()
    for k in range(1, n):
        pl.semaphore_signal(barrier, inc=1, device_id={"pix": me ^ k}, device_id_type=MESH)

    def load(y):
        cols = pl.ds(pl.multiple_of(y * width, width), width)
        return pltpu.make_async_copy(sky_ref.at[:, cols], sky.at[y], load_sem.at[y])

    def begin(y, _):
        load(y).start()
        return 0

    lax.fori_loop(0, rows, begin, 0)
    pl.semaphore_wait(barrier, n - 1)

    def chunk(c, _):
        mix = split(mix_ref[pl.ds(pl.multiple_of(c * step, step), step), :])
        dx = (dxh_ref[...], dxl_ref[...])

        def part(g, _):
            def row(i, _):
                y = g * group + i

                @pl.when(c == 0)
                def _():
                    load(y).wait()
                    h, l = split(sky[y])
                    high[y] = h
                    low[y] = l

                field = dot3(mix, (high[y], low[y])) * mask_ref[y]
                moved = dot3(split(field), dx)
                for p in range(n):
                    for h in range(width // LANES):
                        at = pl.ds(pl.multiple_of(y * tall + h * 8, 8), 8)
                        out[c, p, at, :] = moved[p * 8 : (p + 1) * 8, h * LANES : (h + 1) * LANES]
                return 0

            lax.fori_loop(0, group, row, 0)
            size = group * tall
            here = pl.ds(pl.multiple_of(g * size, size), size)
            there = pl.ds(pl.multiple_of(me * rows * tall + g * size, size), size)
            for k in range(1, n):
                pltpu.make_async_remote_copy(
                    src_ref=out.at[c, me ^ k, here],
                    dst_ref=z_ref.at[c, there],
                    send_sem=send_sem.at[c],
                    recv_sem=recv_sem.at[c],
                    device_id={"pix": me ^ k},
                    device_id_type=MESH,
                ).start()
            pltpu.make_async_copy(out.at[c, me, here], z_ref.at[c, there], own_sem.at[c]).start()
            return 0

        lax.fori_loop(0, rows // group, part, 0)
        return 0

    lax.fori_loop(0, chunks, chunk, 0)

    def finish(c, _):
        got = z_ref.at[c, pl.ds(0, (n - 1) * rows * tall)]
        pltpu.make_async_copy(got, got, send_sem.at[c]).wait()
        pltpu.make_async_copy(got, got, recv_sem.at[c]).wait()
        own = z_ref.at[c, pl.ds(0, rows * tall)]
        pltpu.make_async_copy(own, own, own_sem.at[c]).wait()
        return 0

    lax.fori_loop(0, chunks, finish, 0)


def spread(sky, mask, mix, n):
    channels, pixels = sky.shape
    rows = pixels // SX
    tall = 8 * SX // LANES
    chunks = mix.shape[0] // (8 * n)
    dxh, dxl = split_table(packed_x(SX))
    vmem = pl.BlockSpec(memory_space=pltpu.VMEM)
    hbm = pl.BlockSpec(memory_space=pl.ANY)
    return pl.pallas_call(
        functools.partial(spread_kernel, n),
        out_shape=jax.ShapeDtypeStruct((chunks, n * rows * tall, LANES), jnp.float32),
        in_specs=[hbm, vmem, vmem, vmem, vmem],
        out_specs=hbm,
        scratch_shapes=[
            pltpu.VMEM((rows, channels, SX), jnp.float32),
            pltpu.VMEM((rows, channels, SX), jnp.bfloat16),
            pltpu.VMEM((rows, channels, SX), jnp.bfloat16),
            pltpu.VMEM((chunks, n, rows * tall, LANES), jnp.float32),
            pltpu.SemaphoreType.DMA((rows,)),
            pltpu.SemaphoreType.DMA((chunks,)),
            pltpu.SemaphoreType.DMA((chunks,)),
            pltpu.SemaphoreType.DMA((chunks,)),
        ],
        compiler_params=pltpu.CompilerParams(
            collective_id=1, has_side_effects=True, vmem_limit_bytes=VMEM_LIMIT
        ),
        name="spread",
    )(sky, mask.reshape(rows, 1, SX), mix, dxh, dxl)


def power_kernel(z_ref, dyh_ref, dyl_ref, o_ref, res):
    length = dyh_ref.shape[1]
    half = SX // 2
    dy = (dyh_ref[...], dyl_ref[...])
    lane = lax.broadcasted_iota(jnp.int32, (length, half), 1)
    first = lane == 0
    mirror = jnp.where(first, 0, half - lane)

    def mode(j, _):
        field = [z_ref[0, pl.ds(h * 8 + j, length, stride=16), :] for h in range(2)]
        both = dot3(dy, split(jnp.concatenate(field, axis=1)))
        cc, cs = both[:length, :half], both[:length, half:]
        sc, ss = both[length:, :half], both[length:, half:]
        real = cc - jnp.where(first, 0.0, ss)
        imag = sc + jnp.where(first, 0.0, cs)
        res[pl.ds(j, length, stride=16), :] = real * real + imag * imag
        real = jnp.where(first, 0.0, cc) + ss
        imag = jnp.where(first, 0.0, sc) - cs
        other = real * real + imag * imag
        res[pl.ds(8 + j, length, stride=16), :] = jnp.take_along_axis(other, mirror, axis=1)
        return 0

    for j in range(8):
        mode(j, 0)

    def place(u, _):
        row = res[pl.ds(pl.multiple_of(u * 8, 8), 8), :]
        o_ref[:, pl.ds(pl.multiple_of(u * LANES, LANES), LANES)] = row
        return 0

    lax.fori_loop(0, res.shape[0] // 8, place, 0, unroll=8)


def power_maps(z):
    chunks, tall, _ = z.shape
    length = tall // 16
    dyh, dyl = split_table(full_y(length) / 256.0)
    whole = pl.BlockSpec(dyh.shape, lambda c: (0, 0))
    return pl.pallas_call(
        power_kernel,
        grid=(chunks,),
        out_shape=jax.ShapeDtypeStruct((chunks * 8, length * SX), jnp.float32),
        in_specs=[pl.BlockSpec((1, tall, LANES), lambda c: (c, 0, 0)), whole, whole],
        out_specs=pl.BlockSpec((8, length * SX), lambda c: (c, 0)),
        scratch_shapes=[pltpu.VMEM((tall, LANES), jnp.float32)],
        compiler_params=pltpu.CompilerParams(vmem_limit_bytes=VMEM_LIMIT),
        name="power",
    )(z, dyh, dyl)


def local(sizes, sky_cube, pixel_mask, noise_cov):
    live = pixel_mask[0].astype(jnp.float32)
    masked = sky_cube[0] * live[None, :]
    owners = sizes["pix"]
    share = F // owners
    kernels = share % 8 == 0 and owners & (owners - 1) == 0 and masked.shape[1] % SX == 0 and SX == 2 * LANES
    table = los_table(F)
    if kernels:
        table = table.reshape(owners, share // 8, 8, F).transpose(1, 0, 2, 3).reshape(F, F)
    table = jnp.asarray(table)
    partial_value = jnp.dot(masked, masked.T, precision=MID)
    data_cov = reduce_cov(partial_value, sizes)
    count_all = sizes["pix"] * sizes["rep"] * masked.shape[1]
    folded = folded_transpose(data_cov, 1.0 / count_all, noise_cov, table).T
    if kernels:
        return power_maps(spread(sky_cube[0], live, folded, owners))[None]
    eighth = share // 8
    widths = [eighth, 2 * eighth, 2 * eighth, 2 * eighth, eighth] if eighth else [share]
    by_owner = folded.reshape(owners, share, F)
    result, planes = None, []

    def place(done, at, result):
        power = sky_power(planes[done][0], SY, SX)
        if result is None:
            return jnp.pad(power, ((at, share - at - power.shape[0]), (0, 0)))
        return lax.dynamic_update_slice(result, power, (at, 0))

    starts = [sum(widths[:c]) for c in range(len(widths))]
    for c, width in enumerate(widths):
        rows = by_owner[:, starts[c] : starts[c] + width].reshape(owners * width, F)
        spectra = jnp.dot(rows, masked, precision=MID)
        stacked = spectra.reshape(owners, width, spectra.shape[1])
        if c >= 2:
            result = place(c - 2, starts[c - 2], result)
            stacked, result = lax.optimization_barrier((stacked, result))
        planes.append(lax.all_to_all(stacked, "pix", split_axis=0, concat_axis=2, tiled=True))
    for done in range(max(0, len(widths) - 2), len(widths)):
        result = place(done, starts[done], result)
    return result[None]


def solution(mesh):
    placed = (P("rep", None, "pix"), P("rep", "pix"), P())
    return jax.shard_map(
        functools.partial(local, dict(mesh.shape)),
        mesh=mesh,
        in_specs=placed,
        out_specs=P("rep", "pix", None),
        check_vma=False,
    )
```

```python
import functools
import math

import jax
import jax.numpy as jnp
import ml_dtypes
import numpy as np
from jax import lax
from jax.experimental import pallas as pl
from jax.experimental.pallas import tpu as pltpu
from jax.sharding import PartitionSpec as P

F = 512
SY = 256
SX = 256
BLOCK = 128
GROUP = 8
COV_PIXELS = 2048
LANES = 128
VMEM_LIMIT = 60 * 1024 * 1024

HI = lax.Precision.HIGHEST
MID = lax.Precision.HIGH
MESH = pl.DeviceIdType.MESH


def dft_pair(length):
    idx = jnp.arange(length, dtype=jnp.int32)
    phase = (idx[:, None] * idx[None, :] % length).astype(jnp.float32) * (2.0 * math.pi / length)
    return (jnp.cos(phase), jnp.sin(phase))


def los_table(length):
    idx = np.arange(length)
    half_len = length // 2
    freq = np.where(idx <= half_len, idx, idx - half_len)
    phase = (freq[:, None] * idx[None, :] % length) * (2.0 * math.pi / length)
    values = np.where((idx <= half_len)[:, None], np.cos(phase), np.sin(phase))
    edge = np.logical_or(idx == 0, idx == half_len)
    scale = np.where(edge, math.sqrt(1.0 / length), math.sqrt(2.0 / length))
    return (values * scale[:, None]).astype(np.float32)


def sky_power(planes, rows_y, cols_x):
    count = planes.shape[0]
    field = planes.reshape(count, rows_y, cols_x)
    cos_x, sin_x = dft_pair(cols_x)
    cos_y, sin_y = dft_pair(rows_y)
    both_x = jnp.concatenate([cos_x, sin_x], axis=1)
    both_y = jnp.concatenate([cos_y, sin_y], axis=0)
    first = jnp.einsum("kyx,xw->kyw", field, both_x, precision=MID)
    second = jnp.einsum("vy,kyw->kvw", both_y, first, precision=MID)
    real_part = second[:, :rows_y, :cols_x] - second[:, rows_y:, cols_x:]
    imag_part = -(second[:, rows_y:, :cols_x] + second[:, :rows_y, cols_x:])
    power_map = (real_part * real_part + imag_part * imag_part) / float(rows_y * cols_x)
    return power_map.reshape(count, rows_y * cols_x)


def sum_kernel(axes, x_ref, o_ref, acc, full, got, send_sem, recv_sem):
    where = {name: lax.axis_index(name) for name, _ in axes}
    steps = []
    for name, size in axes:
        bit = 1
        while bit < size:
            steps.append((name, bit))
            bit *= 2

    def partner(name, bit):
        me = where[name]
        mine = lax.rem(me // bit, 2)
        return mine, {name: me + bit * (1 - 2 * mine)}

    barrier = pltpu.get_barrier_semaphore()
    for name, bit in steps:
        _, other = partner(name, bit)
        pl.semaphore_signal(barrier, inc=1, device_id=other, device_id_type=MESH)
    pl.semaphore_wait(barrier, len(steps))

    total = x_ref.shape[0]
    rows, start, offset = total, 0, 0
    acc[...] = x_ref[...]
    plan = []
    for n, (name, bit) in enumerate(steps):
        mine, other = partner(name, bit)
        split = rows % 16 == 0
        if split:
            rows //= 2
            away = start + (1 - mine) * rows
            start = start + mine * rows
        else:
            away = start
        plan.append((other, split, start, rows, mine))
        if split:
            away = pl.multiple_of(away, 8)
        here = pl.multiple_of(start, 8)
        source = x_ref if n == 0 else acc
        copy = pltpu.make_async_remote_copy(
            src_ref=source.at[pl.ds(away, rows)],
            dst_ref=got.at[pl.ds(offset, rows)],
            send_sem=send_sem.at[n],
            recv_sem=recv_sem.at[n],
            device_id=other,
            device_id_type=MESH,
        )
        copy.start()
        copy.wait()
        acc[pl.ds(here, rows)] = acc[pl.ds(here, rows)] + got[pl.ds(offset, rows)]
        offset += rows
    last = pl.ds(pl.multiple_of(start, 8), rows)
    full[last] = acc[last]
    for n in reversed(range(len(steps))):
        other, split, start, rows, mine = plan[n]
        if not split:
            continue
        here = pl.multiple_of(start, 8)
        copy = pltpu.make_async_remote_copy(
            src_ref=full.at[pl.ds(here, rows)],
            dst_ref=full.at[pl.ds(here, rows)],
            send_sem=send_sem.at[len(steps) + n],
            recv_sem=recv_sem.at[len(steps) + n],
            device_id=other,
            device_id_type=MESH,
        )
        copy.start()
        copy.wait()
    o_ref[...] = full[...]


def reduce_cov(partial_value, sizes):
    axes = [("rep", sizes["rep"]), ("pix", sizes["pix"])]
    rows, depth, count = partial_value.shape[0], 0, 0
    for _, size in axes:
        for _ in range(size.bit_length() - 1):
            if rows % 16 == 0:
                rows //= 2
            depth += rows
            count += 1
    vmem = pl.BlockSpec(memory_space=pltpu.VMEM)
    return pl.pallas_call(
        functools.partial(sum_kernel, axes),
        out_shape=jax.ShapeDtypeStruct(partial_value.shape, jnp.float32),
        in_specs=[vmem],
        out_specs=vmem,
        scratch_shapes=[
            pltpu.VMEM(partial_value.shape, jnp.float32),
            pltpu.VMEM(partial_value.shape, jnp.float32),
            pltpu.VMEM((depth, partial_value.shape[1]), jnp.float32),
            pltpu.SemaphoreType.DMA((2 * count,)),
            pltpu.SemaphoreType.DMA((2 * count,)),
        ],
        compiler_params=pltpu.CompilerParams(collective_id=0, has_side_effects=True),
        name="cov_sum",
    )(partial_value)


def tree_sum(terms):
    while len(terms) > 1:
        terms = [a + b for a, b in zip(terms[::2], terms[1::2])]
    return terms[0]


def splat_inverse(d):
    d = [list(r) for r in d]
    n = len(d)
    at = lambda i, j: d[min(i, j)][max(i, j)]
    for k in range(0, n, 2):
        p, q, r = d[k][k], d[k][k + 1], d[k + 1][k + 1]
        scale = 1.0 / (p * r - q * q)
        pi, qi, ri = r * scale, -(q * scale), p * scale
        others = [i for i in range(n) if i not in (k, k + 1)]
        left = {i: (at(i, k), at(i, k + 1)) for i in others}
        new = {i: (left[i][0] * pi + left[i][1] * qi, left[i][0] * qi + left[i][1] * ri) for i in others}
        for i in others:
            for j in others:
                if j >= i:
                    d[i][j] = d[i][j] - (new[i][0] * left[j][0] + new[i][1] * left[j][1])
        for i in others:
            for s in range(2):
                d[min(i, k + s)][max(i, k + s)] = new[i][s]
        d[k][k], d[k][k + 1], d[k + 1][k + 1] = -pi, -qi, -ri
    return d


def block_inverse(a, splat=splat_inverse):
    size = a.shape[0]
    shape = (8, size)
    lane = lax.broadcasted_iota(jnp.int32, shape, 1)
    sub = lax.broadcasted_iota(jnp.int32, shape, 0)
    rows = [a[8 * r : 8 * r + 8, :] for r in range(size // 8)]
    wide = lambda x: jnp.broadcast_to(x, shape)
    for t in range(size // 8):
        own = rows[t]
        cols = [wide(own[:, 8 * t + j : 8 * t + j + 1]) for j in range(8)]
        block = [[wide(cols[j][i : i + 1, :]) if j >= i else None for j in range(8)] for i in range(8)]
        minus = splat(block)
        inside = jnp.logical_and(lane >= 8 * t, lane < 8 * t + 8)
        fixed = jnp.where(inside, (lane - 8 * t == sub).astype(jnp.float32), own)
        base = [wide(fixed[s : s + 1, :]) for s in range(8)]
        new = [tree_sum([minus[min(s, m)][max(s, m)] * base[m] for m in range(8)]) for s in range(8)]
        for r in range(size // 8):
            if r == t:
                out = new[0]
                for s in range(1, 8):
                    out = jnp.where(sub == s, new[s], out)
                rows[r] = -out
            else:
                old = rows[r]
                terms = [wide(old[:, 8 * t + s : 8 * t + s + 1]) * new[s] for s in range(8)]
                rows[r] = jnp.where(inside, 0.0, old) + tree_sum(terms)
    return jnp.concatenate(rows, axis=0)

def solve_kernel(scale, cov_ref, noise_ref, table_ref, o_ref, a_ref):
    size = cov_ref.shape[0]
    blocks = size // BLOCK
    dot = functools.partial(lax.dot_general, precision=HI, preferred_element_type=jnp.float32)

    def mul(x, y):
        return dot(x, y, (((1,), (0,)), ((), ())))

    def mul_t(x, y):
        return dot(x, y, (((1,), (1,)), ((), ())))

    def span(i, j=None):
        return slice(i * BLOCK, (i + 1 if j is None else j) * BLOCK)

    half = cov_ref[...]
    a_ref[...] = (half + half.T) * scale + noise_ref[...]
    for k in range(blocks):
        inverse = block_inverse(a_ref[span(k), span(k)])
        if k == 0:
            o_ref[...] = mul(table_ref[...], noise_ref[...])
        others = [i % blocks for i in range(k + 1, k + blocks)]
        if k + 1 < blocks:
            panel = mul(inverse, a_ref[span(k), span(k + 1, blocks)])
            for i in others:
                rest = span(k + 1, blocks)
                a_ref[span(i), rest] = a_ref[span(i), rest] - mul(a_ref[span(i), span(k)], panel)
            a_ref[span(k), span(k + 1, blocks)] = panel
        right = mul(o_ref[:, span(k)], inverse)
        for i in others:
            o_ref[:, span(i)] = o_ref[:, span(i)] - mul_t(right, a_ref[span(i), span(k)])
        o_ref[:, span(k)] = right


def filter_rows(half_cov, scale, noise_cov, table):
    vmem = pl.BlockSpec(memory_space=pltpu.VMEM)
    return pl.pallas_call(
        functools.partial(solve_kernel, scale),
        out_shape=jax.ShapeDtypeStruct(half_cov.shape, jnp.float32),
        in_specs=[vmem] * 3,
        out_specs=vmem,
        scratch_shapes=[pltpu.VMEM(half_cov.shape, jnp.float32)],
        compiler_params=pltpu.CompilerParams(vmem_limit_bytes=VMEM_LIMIT),
        name="filter_solve",
    )(half_cov, noise_cov, table)


def split(x):
    high = x.astype(jnp.bfloat16)
    return high, (x - high.astype(jnp.float32)).astype(jnp.bfloat16)


def dot3(left, right):
    (lh, ll), (rh, rl) = left, right
    one = functools.partial(jnp.dot, preferred_element_type=jnp.float32)
    return one(lh, rh) + (one(lh, rl) + one(ll, rh))


def split_table(values):
    high = values.astype(ml_dtypes.bfloat16)
    low = (values - high.astype(np.float64)).astype(ml_dtypes.bfloat16)
    return jnp.asarray(high), jnp.asarray(low)


def packed_x(length):
    idx = np.arange(length)
    half = length // 2
    phase = lambda freq: (idx[:, None] * freq[None, :] % length) * (2.0 * math.pi / length)
    cosines = np.cos(phase(np.arange(half + 1)))
    sines = np.sin(phase(np.arange(1, half)))
    return np.concatenate([cosines, sines], axis=1)


def full_y(length):
    idx = np.arange(length)
    phase = (idx[:, None] * idx[None, :] % length) * (2.0 * math.pi / length)
    return np.concatenate([np.cos(phase), np.sin(phase)], axis=0)


def cov_kernel(sky_ref, mask_ref, o_ref):
    high, low = split(sky_ref[...] * mask_ref[...])
    mid = high.shape[0] // 2
    top, low_half = high[:mid], high[mid:]

    def dot(x, y):
        return lax.dot_general(x, y, (((1,), (1,)), ((), ())), preferred_element_type=jnp.float32)

    @pl.when(pl.program_id(0) == 0)
    def _():
        o_ref[...] = jnp.zeros_like(o_ref)

    cross = dot(high, low)
    o_ref[:mid, :mid] = o_ref[:mid, :mid] + (cross[:mid, :mid] + dot(top * 0.5, top))
    o_ref[:mid, mid:] = o_ref[:mid, mid:] + cross[:mid, mid:]
    o_ref[mid:, :mid] = o_ref[mid:, :mid] + (cross[mid:, :mid] + dot(low_half, top))
    o_ref[mid:, mid:] = o_ref[mid:, mid:] + (cross[mid:, mid:] + dot(low_half * 0.5, low_half))


def half_covariance(sky, mask):
    channels, pixels = sky.shape
    width = math.gcd(pixels, COV_PIXELS)
    return pl.pallas_call(
        cov_kernel,
        grid=(pixels // width,),
        out_shape=jax.ShapeDtypeStruct((channels, channels), jnp.float32),
        in_specs=[
            pl.BlockSpec((channels, width), lambda i: (0, i)),
            pl.BlockSpec((1, width), lambda i: (0, i)),
        ],
        out_specs=pl.BlockSpec((channels, channels), lambda i: (0, 0)),
        compiler_params=pltpu.CompilerParams(vmem_limit_bytes=VMEM_LIMIT),
        name="covariance",
    )(sky, mask)


def spread_kernel(
    n, sky_ref, mask_ref, mix_ref, dxh_ref, dxl_ref, dyh_ref, dyl_ref, q_ref,
    stage, high, low, out, z, maps, load_sem, send_sem, recv_sem, own_sem, put_sem,
):
    me = lax.axis_index("pix")
    rows, _, width = high.shape
    chunks = out.shape[0]
    slots = stage.shape[0]
    group = math.gcd(rows, GROUP)
    step = n * 8
    tall = 8 * width // LANES
    length = n * rows

    barrier = pltpu.get_barrier_semaphore()
    for k in range(1, n):
        pl.semaphore_signal(barrier, inc=1, device_id={"pix": me ^ k}, device_id_type=MESH)

    def load(y):
        cols = pl.ds(pl.multiple_of(y * width, width), width)
        slot = lax.rem(y, slots)
        return pltpu.make_async_copy(sky_ref.at[:, cols], stage.at[slot], load_sem.at[slot])

    for y in range(min(slots, rows)):
        load(y).start()
    pl.semaphore_wait(barrier, n - 1)

    def chunk(c, _):
        mix = split(mix_ref[pl.ds(pl.multiple_of(c * step, step), step), :])
        dx = (dxh_ref[...], dxl_ref[...])

        def part(g, _):
            def row(i, _):
                y = g * group + i

                @pl.when(c == 0)
                def _():
                    load(y).wait()
                    h, l = split(stage[lax.rem(y, slots)])
                    high[y] = h
                    low[y] = l

                    @pl.when(y + slots < rows)
                    def _():
                        load(y + slots).start()

                field = dot3(mix, (high[y], low[y])) * mask_ref[y]
                moved = dot3(split(field), dx)
                for p in range(n):
                    for h in range(width // LANES):
                        at = pl.ds(pl.multiple_of(y * tall + h * 8, 8), 8)
                        out[c, p, at, :] = moved[p * 8 : (p + 1) * 8, h * LANES : (h + 1) * LANES]
                return 0

            lax.fori_loop(0, group, row, 0)
            size = group * tall
            here = pl.ds(pl.multiple_of(g * size, size), size)
            there = pl.ds(pl.multiple_of(me * rows * tall + g * size, size), size)
            for k in range(1, n):
                pltpu.make_async_remote_copy(
                    src_ref=out.at[c, me ^ k, here],
                    dst_ref=z.at[c, there],
                    send_sem=send_sem.at[c],
                    recv_sem=recv_sem.at[c],
                    device_id={"pix": me ^ k},
                    device_id_type=MESH,
                ).start()
            pltpu.make_async_copy(out.at[c, me, here], z.at[c, there], own_sem.at[c]).start()
            return 0

        lax.fori_loop(0, rows // group, part, 0)
        return 0

    lax.fori_loop(0, chunks, chunk, 0)

    dy = (dyh_ref[...], dyl_ref[...])
    half = width // 2
    lane = lax.broadcasted_iota(jnp.int32, (length, half), 1)
    row_id = lax.broadcasted_iota(jnp.int32, (length, half), 0)
    first = lane == 0
    late = jnp.logical_and(first, row_id > length // 2)

    def put(c):
        slot = lax.rem(c, 2)
        return pltpu.make_async_copy(maps.at[slot], q_ref.at[c], put_sem.at[slot])

    def finish(c, _):
        others = z.at[c, pl.ds(0, (n - 1) * rows * tall)]
        own = z.at[c, pl.ds(0, rows * tall)]
        pltpu.make_async_copy(others, others, recv_sem.at[c]).wait()
        pltpu.make_async_copy(own, own, own_sem.at[c]).wait()
        slot = lax.rem(c, 2)

        @pl.when(c >= 2)
        def _():
            put(c - 2).wait()

        for j in range(8):
            field = [z[c, pl.ds(h * 8 + j, length, stride=16), :] for h in range(2)]
            both = dot3(dy, split(jnp.concatenate(field, axis=1)))
            cc, cs = both[:length, :half], both[:length, half:]
            sc, ss = both[length:, :half], both[length:, half:]
            real = jnp.where(late, cs, cc - jnp.where(first, 0.0, ss))
            imag = jnp.where(late, ss, sc + jnp.where(first, 0.0, cs))
            maps[slot, pl.ds(j, length, stride=8), :] = real * real + imag * imag
            for e, u in enumerate((0, length // 2)):
                edge = cs[u : u + 1] * cs[u : u + 1] + ss[u : u + 1] * ss[u : u + 1]
                maps[slot, pl.ds((length + e) * 8 + j, 1), :] = edge
        put(c).start()
        return 0

    lax.fori_loop(0, chunks, finish, 0)
    for c in range(max(0, chunks - 2), chunks):
        put(c).wait()

    def sent(c, _):
        others = z.at[c, pl.ds(0, (n - 1) * rows * tall)]
        pltpu.make_async_copy(others, others, send_sem.at[c]).wait()
        return 0

    lax.fori_loop(0, chunks, sent, 0)


def spread(sky, mask, mix, n):
    channels, pixels = sky.shape
    rows = pixels // SX
    tall = 8 * SX // LANES
    chunks = mix.shape[0] // (8 * n)
    dxh, dxl = split_table(packed_x(SX))
    dyh, dyl = split_table(full_y(n * rows) / 256.0)
    vmem = pl.BlockSpec(memory_space=pltpu.VMEM)
    hbm = pl.BlockSpec(memory_space=pl.ANY)
    return pl.pallas_call(
        functools.partial(spread_kernel, n),
        out_shape=jax.ShapeDtypeStruct((chunks, (n * rows + 2) * 8, LANES), jnp.float32),
        in_specs=[hbm] + [vmem] * 6,
        out_specs=hbm,
        scratch_shapes=[
            pltpu.VMEM((4, channels, SX), jnp.float32),
            pltpu.VMEM((rows, channels, SX), jnp.bfloat16),
            pltpu.VMEM((rows, channels, SX), jnp.bfloat16),
            pltpu.VMEM((chunks, n, rows * tall, LANES), jnp.float32),
            pltpu.VMEM((chunks, n * rows * tall, LANES), jnp.float32),
            pltpu.VMEM((2, (n * rows + 2) * 8, LANES), jnp.float32),
            pltpu.SemaphoreType.DMA((4,)),
            pltpu.SemaphoreType.DMA((chunks,)),
            pltpu.SemaphoreType.DMA((chunks,)),
            pltpu.SemaphoreType.DMA((chunks,)),
            pltpu.SemaphoreType.DMA((2,)),
        ],
        compiler_params=pltpu.CompilerParams(
            collective_id=1, has_side_effects=True, vmem_limit_bytes=VMEM_LIMIT
        ),
        name="spread",
    )(sky, mask.reshape(rows, 1, SX), mix, dxh, dxl, dyh, dyl)


def unfold_kernel(q_ref, o_ref):
    length = q_ref.shape[1] // 8 - 2
    shape = (8, LANES)
    lane = lax.broadcasted_iota(jnp.int32, shape, 1)
    first = lane == 0
    mirror = jnp.where(first, 0, LANES - lane)

    def tile(u):
        return q_ref[0, u * 8 : u * 8 + 8, :]

    def back(x):
        return jnp.take_along_axis(x, mirror, axis=1)

    def write(u, near, far):
        o_ref[:, u * SX : u * SX + LANES] = near
        o_ref[:, u * SX + LANES : (u + 1) * SX] = far

    for e, u in enumerate((0, length // 2)):
        a = tile(u)
        write(u, a, jnp.where(first, tile(length + e), back(a)))
    for u in range(1, length // 2):
        v = length - u
        a, b = tile(u), tile(v)
        write(u, a, back(b))
        write(v, jnp.where(first, a, b), jnp.where(first, b, back(a)))


def unfold(q):
    chunks, tall, _ = q.shape
    length = tall // 8 - 2
    return pl.pallas_call(
        unfold_kernel,
        grid=(chunks,),
        out_shape=jax.ShapeDtypeStruct((chunks * 8, length * SX), jnp.float32),
        in_specs=[pl.BlockSpec((1, tall, LANES), lambda c: (c, 0, 0))],
        out_specs=pl.BlockSpec((8, length * SX), lambda c: (c, 0)),
        compiler_params=pltpu.CompilerParams(vmem_limit_bytes=VMEM_LIMIT),
        name="unfold",
    )(q)


def local(sizes, sky_cube, pixel_mask, noise_cov):
    live = pixel_mask[0].astype(jnp.float32)
    masked = sky_cube[0] * live[None, :]
    owners = sizes["pix"]
    share = F // owners
    kernels = share % 8 == 0 and owners & (owners - 1) == 0 and masked.shape[1] % SX == 0 and SX == 2 * LANES
    table = los_table(F)
    if kernels:
        table = table.reshape(owners, share // 8, 8, F).transpose(1, 0, 2, 3).reshape(F, F)
    table = jnp.asarray(table)
    data_cov = reduce_cov(half_covariance(sky_cube[0], live[None, :]), sizes)
    count_all = sizes["pix"] * sizes["rep"] * masked.shape[1]
    folded = filter_rows(data_cov, 1.0 / count_all, noise_cov, table)
    if kernels:
        return unfold(spread(sky_cube[0], live, folded, owners))[None]
    eighth = share // 8
    widths = [eighth, 2 * eighth, 2 * eighth, 2 * eighth, eighth] if eighth else [share]
    by_owner = folded.reshape(owners, share, F)
    result, planes = None, []

    def place(done, at, result):
        power = sky_power(planes[done][0], SY, SX)
        if result is None:
            return jnp.pad(power, ((at, share - at - power.shape[0]), (0, 0)))
        return lax.dynamic_update_slice(result, power, (at, 0))

    starts = [sum(widths[:c]) for c in range(len(widths))]
    for c, width in enumerate(widths):
        rows = by_owner[:, starts[c] : starts[c] + width].reshape(owners * width, F)
        spectra = jnp.dot(rows, masked, precision=MID)
        stacked = spectra.reshape(owners, width, spectra.shape[1])
        if c >= 2:
            result = place(c - 2, starts[c - 2], result)
            stacked, result = lax.optimization_barrier((stacked, result))
        planes.append(lax.all_to_all(stacked, "pix", split_axis=0, concat_axis=2, tiled=True))
    for done in range(max(0, len(widths) - 2), len(widths)):
        result = place(done, starts[done], result)
    return result[None]


def solution(mesh):
    placed = (P("rep", None, "pix"), P("rep", "pix"), P())
    return jax.shard_map(
        functools.partial(local, dict(mesh.shape)),
        mesh=mesh,
        in_specs=placed,
        out_specs=P("rep", "pix", None),
        check_vma=False,
    )
```

```python
import functools
import math

import jax
import jax.numpy as jnp
import ml_dtypes
import numpy as np
from jax import lax
from jax.experimental import pallas as pl
from jax.experimental.pallas import tpu as pltpu
from jax.sharding import PartitionSpec as P

F = 512
SY = 256
SX = 256
BLOCK = 128
GROUP = 3
TURNS = 4
COV_PIXELS = 1024
LANES = 128
VMEM_LIMIT = 52 * 1024 * 1024
SMALL_LIMIT = 24 * 1024 * 1024

HI = lax.Precision.HIGHEST
MID = lax.Precision.HIGH
MESH = pl.DeviceIdType.MESH


def dft_pair(length):
    idx = jnp.arange(length, dtype=jnp.int32)
    phase = (idx[:, None] * idx[None, :] % length).astype(jnp.float32) * (2.0 * math.pi / length)
    return (jnp.cos(phase), jnp.sin(phase))


def los_table(length):
    idx = np.arange(length)
    half_len = length // 2
    freq = np.where(idx <= half_len, idx, idx - half_len)
    phase = (freq[:, None] * idx[None, :] % length) * (2.0 * math.pi / length)
    values = np.where((idx <= half_len)[:, None], np.cos(phase), np.sin(phase))
    edge = np.logical_or(idx == 0, idx == half_len)
    scale = np.where(edge, math.sqrt(1.0 / length), math.sqrt(2.0 / length))
    return (values * scale[:, None]).astype(np.float32)


def sky_power(planes, rows_y, cols_x):
    count = planes.shape[0]
    field = planes.reshape(count, rows_y, cols_x)
    cos_x, sin_x = dft_pair(cols_x)
    cos_y, sin_y = dft_pair(rows_y)
    both_x = jnp.concatenate([cos_x, sin_x], axis=1)
    both_y = jnp.concatenate([cos_y, sin_y], axis=0)
    first = jnp.einsum("kyx,xw->kyw", field, both_x, precision=MID)
    second = jnp.einsum("vy,kyw->kvw", both_y, first, precision=MID)
    real_part = second[:, :rows_y, :cols_x] - second[:, rows_y:, cols_x:]
    imag_part = -(second[:, rows_y:, :cols_x] + second[:, :rows_y, cols_x:])
    power_map = (real_part * real_part + imag_part * imag_part) / float(rows_y * cols_x)
    return power_map.reshape(count, rows_y * cols_x)


def sum_kernel(axes, x_ref, o_ref, acc, full, got, send_sem, recv_sem):
    where = {name: lax.axis_index(name) for name, _ in axes}
    steps = []
    for name, size in axes:
        bit = 1
        while bit < size:
            steps.append((name, bit))
            bit *= 2

    def partner(name, bit):
        me = where[name]
        mine = lax.rem(me // bit, 2)
        return mine, {name: me + bit * (1 - 2 * mine)}

    barrier = pltpu.get_barrier_semaphore()
    for name, bit in steps:
        _, other = partner(name, bit)
        pl.semaphore_signal(barrier, inc=1, device_id=other, device_id_type=MESH)
    pl.semaphore_wait(barrier, len(steps))

    total = x_ref.shape[0]
    rows, start, offset = total, 0, 0
    acc[...] = x_ref[...]
    plan = []
    for n, (name, bit) in enumerate(steps):
        mine, other = partner(name, bit)
        split = rows % 16 == 0
        if split:
            rows //= 2
            away = start + (1 - mine) * rows
            start = start + mine * rows
        else:
            away = start
        plan.append((other, split, start, rows, mine))
        if split:
            away = pl.multiple_of(away, 8)
        here = pl.multiple_of(start, 8)
        source = x_ref if n == 0 else acc
        copy = pltpu.make_async_remote_copy(
            src_ref=source.at[pl.ds(away, rows)],
            dst_ref=got.at[pl.ds(offset, rows)],
            send_sem=send_sem.at[n],
            recv_sem=recv_sem.at[n],
            device_id=other,
            device_id_type=MESH,
        )
        copy.start()
        copy.wait()
        acc[pl.ds(here, rows)] = acc[pl.ds(here, rows)] + got[pl.ds(offset, rows)]
        offset += rows
    last = pl.ds(pl.multiple_of(start, 8), rows)
    full[last] = acc[last]
    for n in reversed(range(len(steps))):
        other, split, start, rows, mine = plan[n]
        if not split:
            continue
        here = pl.multiple_of(start, 8)
        copy = pltpu.make_async_remote_copy(
            src_ref=full.at[pl.ds(here, rows)],
            dst_ref=full.at[pl.ds(here, rows)],
            send_sem=send_sem.at[len(steps) + n],
            recv_sem=recv_sem.at[len(steps) + n],
            device_id=other,
            device_id_type=MESH,
        )
        copy.start()
        copy.wait()
    o_ref[...] = full[...]


def reduce_cov(partial_value, sizes):
    axes = [("rep", sizes["rep"]), ("pix", sizes["pix"])]
    rows, depth, count = partial_value.shape[0], 0, 0
    for _, size in axes:
        for _ in range(size.bit_length() - 1):
            if rows % 16 == 0:
                rows //= 2
            depth += rows
            count += 1
    vmem = pl.BlockSpec(memory_space=pltpu.VMEM)
    return pl.pallas_call(
        functools.partial(sum_kernel, axes),
        out_shape=jax.ShapeDtypeStruct(partial_value.shape, jnp.float32),
        in_specs=[vmem],
        out_specs=vmem,
        scratch_shapes=[
            pltpu.VMEM(partial_value.shape, jnp.float32),
            pltpu.VMEM(partial_value.shape, jnp.float32),
            pltpu.VMEM((depth, partial_value.shape[1]), jnp.float32),
            pltpu.SemaphoreType.DMA((2 * count,)),
            pltpu.SemaphoreType.DMA((2 * count,)),
        ],
        compiler_params=pltpu.CompilerParams(collective_id=0, has_side_effects=True),
        name="cov_sum",
    )(partial_value)


def lower_blocks(size):
    return [(i, j) for i in range(size // BLOCK) for j in range(i + 1)]


def stage_sum_kernel(stages, x_ref, o_ref, acc, full, got, send_sem, recv_sem):
    where = {name: lax.axis_index(name) for name in ("pix", "rep")}
    blocks = lower_blocks(x_ref.shape[0])

    def span(i):
        return slice(i * BLOCK, (i + 1) * BLOCK)

    def partner(stage, e):
        moved = dict(where)
        for b, (name, bit) in enumerate(stage):
            if e >> b & 1:
                moved[name] = moved[name] ^ bit
        return {name: moved[name] for name in {name for name, _ in stage}}

    def place(stage):
        index = 0
        for b, (name, bit) in enumerate(stage):
            index = index + (where[name] // bit % 2) * 2**b
        return index

    barrier = pltpu.get_barrier_semaphore()
    count = 0
    for stage in stages:
        for e in range(1, 2 ** len(stage)):
            pl.semaphore_signal(barrier, inc=1, device_id=partner(stage, e), device_id_type=MESH)
            count += 1
    for n, (i, j) in enumerate(blocks):
        acc[span(n)] = x_ref[span(i), span(j)] + x_ref[span(j), span(i)].T
    pl.semaphore_wait(barrier, count)

    rows, start, offset, sem = acc.shape[0], 0, 0, 0
    plan, sends = [], []
    for stage in stages:
        members = 2 ** len(stage)
        rows //= members
        index = place(stage)
        copies = []
        for e in range(1, members):
            away = pl.multiple_of(start + (index ^ e) * rows, 8)
            copies.append(
                pltpu.make_async_remote_copy(
                    src_ref=acc.at[pl.ds(away, rows)],
                    dst_ref=got.at[pl.ds(offset + (e - 1) * rows, rows)],
                    send_sem=send_sem.at[sem],
                    recv_sem=recv_sem.at[sem],
                    device_id=partner(stage, e),
                    device_id_type=MESH,
                )
            )
            copies[-1].start()
            sem += 1
        start = start + index * rows
        here = pl.ds(pl.multiple_of(start, 8), rows)
        total = acc[here]
        for e, copy in enumerate(copies):
            copy.wait_recv()
            total = total + got[offset + e * rows : offset + (e + 1) * rows]
        acc[here] = total
        plan.append((stage, start, rows))
        sends += copies
        offset += (members - 1) * rows
    full[here] = total
    for stage, start, rows in reversed(plan):
        here = pl.ds(pl.multiple_of(start, 8), rows)
        copies = []
        for e in range(1, 2 ** len(stage)):
            copies.append(
                pltpu.make_async_remote_copy(
                    src_ref=full.at[here],
                    dst_ref=full.at[here],
                    send_sem=send_sem.at[sem],
                    recv_sem=recv_sem.at[sem],
                    device_id=partner(stage, e),
                    device_id_type=MESH,
                )
            )
            copies[-1].start()
            sem += 1
        for copy in copies:
            copy.wait_recv()
        sends += copies
    for n, (i, j) in enumerate(blocks):
        o_ref[span(i), span(j)] = full[span(n)]
        if i != j:
            o_ref[span(j), span(i)] = full[span(n)].T
    for copy in sends:
        copy.wait_send()


def stage_bits(name, size):
    return [(name, 2**b) for b in range(size.bit_length() - 1)]


def sum_both(half, sizes):
    rep, pix = stage_bits("rep", sizes["rep"]), stage_bits("pix", sizes["pix"])
    stages = [s for s in (rep[:1], rep[1:] + pix[:1], pix[1:]) if s]
    size = half.shape[0]
    rows = len(lower_blocks(size)) * BLOCK
    if rows % (8 * sizes["rep"] * sizes["pix"]):
        total = reduce_cov(half, sizes)
        return total + total.T
    count = sum(2 ** len(stage) - 1 for stage in stages)
    vmem = pl.BlockSpec(memory_space=pltpu.VMEM)
    return pl.pallas_call(
        functools.partial(stage_sum_kernel, stages),
        out_shape=jax.ShapeDtypeStruct(half.shape, jnp.float32),
        in_specs=[vmem],
        out_specs=vmem,
        scratch_shapes=[
            pltpu.VMEM((rows, BLOCK), jnp.float32),
            pltpu.VMEM((rows, BLOCK), jnp.float32),
            pltpu.VMEM((rows, BLOCK), jnp.float32),
            pltpu.SemaphoreType.DMA((2 * count,)),
            pltpu.SemaphoreType.DMA((2 * count,)),
        ],
        compiler_params=pltpu.CompilerParams(
            collective_id=0, has_side_effects=True, vmem_limit_bytes=16 * 1024 * 1024
        ),
        name="cov_sum",
    )(half)


def tree_sum(terms):
    while len(terms) > 1:
        terms = [a + b for a, b in zip(terms[::2], terms[1::2])]
    return terms[0]


def splat_inverse(d):
    d = [list(r) for r in d]
    n = len(d)
    at = lambda i, j: d[min(i, j)][max(i, j)]
    for k in range(0, n, 2):
        p, q, r = d[k][k], d[k][k + 1], d[k + 1][k + 1]
        scale = 1.0 / (p * r - q * q)
        pi, qi, ri = r * scale, -(q * scale), p * scale
        others = [i for i in range(n) if i not in (k, k + 1)]
        left = {i: (at(i, k), at(i, k + 1)) for i in others}
        new = {i: (left[i][0] * pi + left[i][1] * qi, left[i][0] * qi + left[i][1] * ri) for i in others}
        for i in others:
            for j in others:
                if j >= i:
                    d[i][j] = d[i][j] - (new[i][0] * left[j][0] + new[i][1] * left[j][1])
        for i in others:
            for s in range(2):
                d[min(i, k + s)][max(i, k + s)] = new[i][s]
        d[k][k], d[k][k + 1], d[k + 1][k + 1] = -pi, -qi, -ri
    return d


def block_inverse(a, splat=splat_inverse):
    size = a.shape[0]
    shape = (8, size)
    lane = lax.broadcasted_iota(jnp.int32, shape, 1)
    sub = lax.broadcasted_iota(jnp.int32, shape, 0)
    rows = [a[8 * r : 8 * r + 8, :] for r in range(size // 8)]
    wide = lambda x: jnp.broadcast_to(x, shape)
    for t in range(size // 8):
        own = rows[t]
        cols = [wide(own[:, 8 * t + j : 8 * t + j + 1]) for j in range(8)]
        block = [[wide(cols[j][i : i + 1, :]) if j >= i else None for j in range(8)] for i in range(8)]
        minus = splat(block)
        inside = jnp.logical_and(lane >= 8 * t, lane < 8 * t + 8)
        fixed = jnp.where(inside, (lane - 8 * t == sub).astype(jnp.float32), own)
        base = [wide(fixed[s : s + 1, :]) for s in range(8)]
        new = [tree_sum([minus[min(s, m)][max(s, m)] * base[m] for m in range(8)]) for s in range(8)]
        for r in range(size // 8):
            if r == t:
                out = new[0]
                for s in range(1, 8):
                    out = jnp.where(sub == s, new[s], out)
                rows[r] = -out
            else:
                old = rows[r]
                terms = [wide(old[:, 8 * t + s : 8 * t + s + 1]) * new[s] for s in range(8)]
                rows[r] = jnp.where(inside, 0.0, old) + tree_sum(terms)
    return jnp.concatenate(rows, axis=0)

def solve_kernel(scale, cov_ref, noise_ref, table_ref, o_ref, a_ref):
    size = cov_ref.shape[0]
    blocks = size // BLOCK
    dot = functools.partial(lax.dot_general, precision=HI, preferred_element_type=jnp.float32)

    def mul(x, y):
        return dot(x, y, (((1,), (0,)), ((), ())))

    def mul_t(x, y):
        return dot(x, y, (((1,), (1,)), ((), ())))

    def span(i, j=None):
        return slice(i * BLOCK, (i + 1 if j is None else j) * BLOCK)

    a_ref[...] = cov_ref[...] * scale + noise_ref[...]
    for k in range(blocks):
        inverse = block_inverse(a_ref[span(k), span(k)])
        if k == 0:
            o_ref[...] = mul(table_ref[...], noise_ref[...])
        others = [i % blocks for i in range(k + 1, k + blocks)]
        if k + 1 < blocks:
            panel = mul(inverse, a_ref[span(k), span(k + 1, blocks)])
            for i in others:
                rest = span(k + 1, blocks)
                a_ref[span(i), rest] = a_ref[span(i), rest] - mul(a_ref[span(i), span(k)], panel)
            a_ref[span(k), span(k + 1, blocks)] = panel
        right = mul(o_ref[:, span(k)], inverse)
        for i in others:
            o_ref[:, span(i)] = o_ref[:, span(i)] - mul_t(right, a_ref[span(i), span(k)])
        o_ref[:, span(k)] = right


def filter_rows(data_cov, scale, noise_cov, table):
    vmem = pl.BlockSpec(memory_space=pltpu.VMEM)
    return pl.pallas_call(
        functools.partial(solve_kernel, scale),
        out_shape=jax.ShapeDtypeStruct(data_cov.shape, jnp.float32),
        in_specs=[vmem] * 3,
        out_specs=vmem,
        scratch_shapes=[pltpu.VMEM(data_cov.shape, jnp.float32)],
        compiler_params=pltpu.CompilerParams(vmem_limit_bytes=SMALL_LIMIT),
        name="filter_solve",
    )(data_cov, noise_cov, table)


def split(x):
    high = x.astype(jnp.bfloat16)
    return high, (x - high.astype(jnp.float32)).astype(jnp.bfloat16)


def dot3(left, right):
    (lh, ll), (rh, rl) = left, right
    one = functools.partial(jnp.dot, preferred_element_type=jnp.float32)
    return one(lh, rh) + (one(lh, rl) + one(ll, rh))


def split_table(values):
    high = values.astype(ml_dtypes.bfloat16)
    low = (values - high.astype(np.float64)).astype(ml_dtypes.bfloat16)
    return jnp.asarray(high), jnp.asarray(low)


def packed_x(length):
    idx = np.arange(length)
    half = length // 2
    phase = lambda freq: (idx[:, None] * freq[None, :] % length) * (2.0 * math.pi / length)
    cosines = np.cos(phase(np.arange(half + 1)))
    sines = np.sin(phase(np.arange(1, half)))
    return np.concatenate([cosines, sines], axis=1)


def full_y(length):
    idx = np.arange(length)
    phase = (idx[:, None] * idx[None, :] % length) * (2.0 * math.pi / length)
    return np.concatenate([np.cos(phase), np.sin(phase)], axis=0)


def cov_kernel(sky_ref, mask_ref, o_ref):
    high, low = split(sky_ref[...] * mask_ref[...].astype(jnp.float32))
    mid = high.shape[0] // 2
    top, low_half = high[:mid], high[mid:]

    def dot(x, y):
        return lax.dot_general(x, y, (((1,), (1,)), ((), ())), preferred_element_type=jnp.float32)

    @pl.when(pl.program_id(0) == 0)
    def _():
        o_ref[...] = jnp.zeros_like(o_ref)

    cross = dot(high, low)
    o_ref[:mid, :mid] = o_ref[:mid, :mid] + (cross[:mid, :mid] + dot(top * 0.5, top))
    o_ref[:mid, mid:] = o_ref[:mid, mid:] + cross[:mid, mid:]
    o_ref[mid:, :mid] = o_ref[mid:, :mid] + (cross[mid:, :mid] + dot(low_half, top))
    o_ref[mid:, mid:] = o_ref[mid:, mid:] + (cross[mid:, mid:] + dot(low_half * 0.5, low_half))


def half_covariance(sky, mask):
    channels, pixels = sky.shape
    width = math.gcd(pixels, COV_PIXELS)
    return pl.pallas_call(
        cov_kernel,
        grid=(pixels // width,),
        out_shape=jax.ShapeDtypeStruct((channels, channels), jnp.float32),
        in_specs=[
            pl.BlockSpec((channels, width), lambda i: (0, i)),
            pl.BlockSpec((1, width), lambda i: (0, i)),
        ],
        out_specs=pl.BlockSpec((channels, channels), lambda i: (0, 0)),
        compiler_params=pltpu.CompilerParams(vmem_limit_bytes=VMEM_LIMIT),
        name="covariance",
    )(sky, mask)


def spread_kernel(
    n, sky_ref, first_ref, second_ref, mask_ref, mix_ref, dxh_ref, dxl_ref, dyh_ref, dyl_ref, q_ref,
    stage, high, low, out, z, maps, load_sem, send_sem, recv_sem, own_sem, put_sem,
):
    me = lax.axis_index("pix")
    entries, _, width = high.shape
    parts = (first_ref, second_ref)
    shared = len(parts)
    rows = entries - shared
    plain = rows - shared
    chunks, turns = z.shape[0], out.shape[0]
    slots = stage.shape[0]
    group = max(d for d in range(1, GROUP + 1) if plain % d == 0)
    side = n // 2
    step = n * 8
    tall = 8 * width // LANES
    length = n * rows
    moved_rows = length - entries

    barrier = pltpu.get_barrier_semaphore()
    for k in range(1, n):
        pl.semaphore_signal(barrier, inc=1, device_id={"pix": me ^ k}, device_id_type=MESH)

    def load(ref, y, i):
        cols = pl.ds(pl.multiple_of(y * width, width), width)
        slot = lax.rem(i, slots)
        return pltpu.make_async_copy(ref.at[:, cols], stage.at[slot], load_sem.at[slot])

    def load_next(i):
        @pl.when(i < rows)
        def _():
            load(sky_ref, lax.rem(i + shared, rows), i).start()

        for e, ref in enumerate(parts):

            @pl.when(i == rows + e)
            def _():
                load(ref, 0, i).start()

    for i in range(slots):
        load(sky_ref, i + shared, i).start()
    pl.semaphore_wait(barrier, n - 1)

    def own_arrived(c):
        own = z.at[c, pl.ds(0, entries * tall)]
        pltpu.make_async_copy(own, own, own_sem.at[c]).wait()

    def others_sent(c):
        others = z.at[c, pl.ds(0, moved_rows * tall)]
        pltpu.make_async_copy(others, others, send_sem.at[c]).wait()

    def chunk(c, _):
        slot = lax.rem(c, turns)

        @pl.when(c >= turns)
        def _():
            own_arrived(c - turns)
            others_sent(c - turns)

        mix = split(mix_ref[pl.ds(pl.multiple_of(c * step, step), step), :])
        dx = (dxh_ref[...], dxl_ref[...])

        def entry(i, _):
            @pl.when(c == 0)
            def _():
                load(sky_ref, 0, i).wait()
                h, l = split(stage[lax.rem(i, slots)])
                high[i] = h
                low[i] = l
                load_next(i + slots)

            live = mask_ref[lax.rem(i + shared, rows)].astype(jnp.float32)
            field = dot3(mix, (high[i], low[i])) * jnp.where(i < rows, live, 1.0)
            moved = dot3(split(field), dx)
            for p in range(n):
                for h in range(width // LANES):
                    at = pl.ds(pl.multiple_of(i * tall + h * 8, 8), 8)
                    out[slot, p, at, :] = moved[p * 8 : (p + 1) * 8, h * LANES : (h + 1) * LANES]
            return 0

        def send(i, y, size, partners):
            here = pl.ds(pl.multiple_of(i * tall, tall), size * tall)
            there = pl.ds(pl.multiple_of(y * tall, tall), size * tall)
            for k in range(1, partners):
                pltpu.make_async_remote_copy(
                    src_ref=out.at[slot, me ^ k, here],
                    dst_ref=z.at[c, there],
                    send_sem=send_sem.at[c],
                    recv_sem=recv_sem.at[c],
                    device_id={"pix": me ^ k},
                    device_id_type=MESH,
                ).start()
            pltpu.make_async_copy(out.at[slot, me, here], z.at[c, there], own_sem.at[c]).start()

        def part(g, _):
            lax.fori_loop(g * group, (g + 1) * group, entry, 0)
            send(g * group, me * rows + shared + g * group, group, n)
            return 0

        lax.fori_loop(0, plain // group, part, 0)
        if shared:
            lax.fori_loop(plain, entries, entry, 0)
            send(plain, me * rows, shared, side)
            send(rows, (me ^ side) * rows, shared, side)
        return 0

    lax.fori_loop(0, chunks, chunk, 0)
    for c in range(chunks - turns, chunks):
        own_arrived(c)

    dy = (dyh_ref[...], dyl_ref[...])
    half = width // 2
    lane = lax.broadcasted_iota(jnp.int32, (length, half), 1)
    row_id = lax.broadcasted_iota(jnp.int32, (length, half), 0)
    first = lane == 0
    late = jnp.logical_and(first, row_id > length // 2)

    def put(c):
        slot = lax.rem(c, 2)
        return pltpu.make_async_copy(maps.at[slot], q_ref.at[c], put_sem.at[slot])

    def finish(c, _):
        others = z.at[c, pl.ds(0, moved_rows * tall)]
        pltpu.make_async_copy(others, others, recv_sem.at[c]).wait()
        slot = lax.rem(c, 2)

        @pl.when(c >= 2)
        def _():
            put(c - 2).wait()

        for j in range(8):
            field = [z[c, pl.ds(h * 8 + j, length, stride=16), :] for h in range(2)]
            both = dot3(dy, split(jnp.concatenate(field, axis=1)))
            cc, cs = both[:length, :half], both[:length, half:]
            sc, ss = both[length:, :half], both[length:, half:]
            real = jnp.where(late, cs, cc - jnp.where(first, 0.0, ss))
            imag = jnp.where(late, ss, sc + jnp.where(first, 0.0, cs))
            maps[slot, pl.ds(j, length, stride=8), :] = real * real + imag * imag
            for e, u in enumerate((0, length // 2)):
                edge = cs[u : u + 1] * cs[u : u + 1] + ss[u : u + 1] * ss[u : u + 1]
                maps[slot, pl.ds((length + e) * 8 + j, 1), :] = edge
        put(c).start()
        return 0

    lax.fori_loop(0, chunks, finish, 0)
    for c in range(max(0, chunks - 2), chunks):
        put(c).wait()

    for c in range(chunks - turns, chunks):
        others_sent(c)


def spread(sky, extras, mask, mix, n):
    channels, pixels = sky.shape
    rows = pixels // SX
    entries = rows + len(extras)
    tall = 8 * SX // LANES
    chunks = mix.shape[0] // (8 * n)
    dxh, dxl = split_table(packed_x(SX))
    dyh, dyl = split_table(full_y(n * rows) / 256.0)
    vmem = pl.BlockSpec(memory_space=pltpu.VMEM)
    hbm = pl.BlockSpec(memory_space=pl.ANY)
    return pl.pallas_call(
        functools.partial(spread_kernel, n),
        out_shape=jax.ShapeDtypeStruct((chunks, (n * rows + 2) * 8, LANES), jnp.float32),
        in_specs=[hbm] * (1 + len(extras)) + [vmem] * 6,
        out_specs=hbm,
        scratch_shapes=[
            pltpu.VMEM((4, channels, SX), jnp.float32),
            pltpu.VMEM((entries, channels, SX), jnp.bfloat16),
            pltpu.VMEM((entries, channels, SX), jnp.bfloat16),
            pltpu.VMEM((min(chunks, TURNS), n, entries * tall, LANES), jnp.float32),
            pltpu.VMEM((chunks, n * rows * tall, LANES), jnp.float32),
            pltpu.VMEM((2, (n * rows + 2) * 8, LANES), jnp.float32),
            pltpu.SemaphoreType.DMA((4,)),
            pltpu.SemaphoreType.DMA((chunks,)),
            pltpu.SemaphoreType.DMA((chunks,)),
            pltpu.SemaphoreType.DMA((chunks,)),
            pltpu.SemaphoreType.DMA((2,)),
        ],
        compiler_params=pltpu.CompilerParams(
            collective_id=1, has_side_effects=True, vmem_limit_bytes=VMEM_LIMIT
        ),
        name="spread",
    )(sky, *extras, mask.reshape(rows, 1, SX), mix, dxh, dxl, dyh, dyl)


def unfold_kernel(q_ref, o_ref):
    length = q_ref.shape[1] // 8 - 2
    shape = (8, LANES)
    lane = lax.broadcasted_iota(jnp.int32, shape, 1)
    first = lane == 0
    mirror = jnp.where(first, 0, LANES - lane)

    def tile(u):
        return q_ref[0, u * 8 : u * 8 + 8, :]

    def back(x):
        return jnp.take_along_axis(x, mirror, axis=1)

    def write(u, near, far):
        o_ref[:, u * SX : u * SX + LANES] = near
        o_ref[:, u * SX + LANES : (u + 1) * SX] = far

    for e, u in enumerate((0, length // 2)):
        a = tile(u)
        write(u, a, jnp.where(first, tile(length + e), back(a)))
    for u in range(1, length // 2):
        v = length - u
        a, b = tile(u), tile(v)
        write(u, a, back(b))
        write(v, jnp.where(first, a, b), jnp.where(first, b, back(a)))


def unfold(q):
    chunks, tall, _ = q.shape
    length = tall // 8 - 2
    return pl.pallas_call(
        unfold_kernel,
        grid=(chunks,),
        out_shape=jax.ShapeDtypeStruct((chunks * 8, length * SX), jnp.float32),
        in_specs=[pl.BlockSpec((1, tall, LANES), lambda c: (c, 0, 0))],
        out_specs=pl.BlockSpec((8, length * SX), lambda c: (c, 0)),
        compiler_params=pltpu.CompilerParams(vmem_limit_bytes=SMALL_LIMIT),
        name="unfold",
    )(q)


def local(sizes, sky_cube, pixel_mask, noise_cov):
    live = pixel_mask[0].astype(jnp.float32)
    masked = sky_cube[0] * live[None, :]
    owners = sizes["pix"]
    share = F // owners
    kernels = share % 8 == 0 and owners & (owners - 1) == 0 and masked.shape[1] % SX == 0 and SX == 2 * LANES
    table = los_table(F)
    if kernels:
        table = table.reshape(owners, share // 8, 8, F).transpose(1, 0, 2, 3).reshape(F, F)
    table = jnp.asarray(table)
    count_all = sizes["pix"] * sizes["rep"] * masked.shape[1]
    if not kernels:
        data_cov = sum_both(half_covariance(sky_cube[0], pixel_mask), sizes)
        folded = filter_rows(data_cov, 1.0 / count_all, noise_cov, table)
    else:
        across = [(p, p ^ (owners // 2)) for p in range(owners)]
        near = sky_cube[0, :, : 2 * SX] * pixel_mask[0, : 2 * SX].astype(jnp.float32)
        near, mask = lax.optimization_barrier((near, pixel_mask))
        first = lax.ppermute(near[:, :SX], "pix", across)
        data_cov = sum_both(half_covariance(sky_cube[0], mask), sizes)
        data_cov, later = lax.optimization_barrier((data_cov, near[:, SX:]))
        second = lax.ppermute(later, "pix", across)
        folded = filter_rows(data_cov, 1.0 / count_all, noise_cov, table)
        return unfold(spread(sky_cube[0], [first, second], pixel_mask, folded, owners))[None]
    eighth = share // 8
    widths = [eighth, 2 * eighth, 2 * eighth, 2 * eighth, eighth] if eighth else [share]
    by_owner = folded.reshape(owners, share, F)
    result, planes = None, []

    def place(done, at, result):
        power = sky_power(planes[done][0], SY, SX)
        if result is None:
            return jnp.pad(power, ((at, share - at - power.shape[0]), (0, 0)))
        return lax.dynamic_update_slice(result, power, (at, 0))

    starts = [sum(widths[:c]) for c in range(len(widths))]
    for c, width in enumerate(widths):
        rows = by_owner[:, starts[c] : starts[c] + width].reshape(owners * width, F)
        spectra = jnp.dot(rows, masked, precision=MID)
        stacked = spectra.reshape(owners, width, spectra.shape[1])
        if c >= 2:
            result = place(c - 2, starts[c - 2], result)
            stacked, result = lax.optimization_barrier((stacked, result))
        planes.append(lax.all_to_all(stacked, "pix", split_axis=0, concat_axis=2, tiled=True))
    for done in range(max(0, len(widths) - 2), len(widths)):
        result = place(done, starts[done], result)
    return result[None]


def solution(mesh):
    placed = (P("rep", None, "pix"), P("rep", "pix"), P())
    return jax.shard_map(
        functools.partial(local, dict(mesh.shape)),
        mesh=mesh,
        in_specs=placed,
        out_specs=P("rep", "pix", None),
        check_vma=False,
    )
```

```python
import functools
import math

import jax
import jax.numpy as jnp
import ml_dtypes
import numpy as np
from jax import lax
from jax.experimental import pallas as pl
from jax.experimental.pallas import tpu as pltpu
from jax.sharding import PartitionSpec as P

F = 512
SY = 256
SX = 256
BLOCK = 128
GROUP = 3
TURNS = 4
COV_PIXELS = 2048
COV_STEP = 512
LANES = 128
VMEM_LIMIT = 52 * 1024 * 1024
SMALL_LIMIT = 24 * 1024 * 1024

HI = lax.Precision.HIGHEST
MID = lax.Precision.HIGH
MESH = pl.DeviceIdType.MESH


def dft_pair(length):
    idx = jnp.arange(length, dtype=jnp.int32)
    phase = (idx[:, None] * idx[None, :] % length).astype(jnp.float32) * (2.0 * math.pi / length)
    return (jnp.cos(phase), jnp.sin(phase))


def los_table(length):
    idx = np.arange(length)
    half_len = length // 2
    freq = np.where(idx <= half_len, idx, idx - half_len)
    phase = (freq[:, None] * idx[None, :] % length) * (2.0 * math.pi / length)
    values = np.where((idx <= half_len)[:, None], np.cos(phase), np.sin(phase))
    edge = np.logical_or(idx == 0, idx == half_len)
    scale = np.where(edge, math.sqrt(1.0 / length), math.sqrt(2.0 / length))
    return (values * scale[:, None]).astype(np.float32)


def sky_power(planes, rows_y, cols_x):
    count = planes.shape[0]
    field = planes.reshape(count, rows_y, cols_x)
    cos_x, sin_x = dft_pair(cols_x)
    cos_y, sin_y = dft_pair(rows_y)
    both_x = jnp.concatenate([cos_x, sin_x], axis=1)
    both_y = jnp.concatenate([cos_y, sin_y], axis=0)
    first = jnp.einsum("kyx,xw->kyw", field, both_x, precision=MID)
    second = jnp.einsum("vy,kyw->kvw", both_y, first, precision=MID)
    real_part = second[:, :rows_y, :cols_x] - second[:, rows_y:, cols_x:]
    imag_part = -(second[:, rows_y:, :cols_x] + second[:, :rows_y, cols_x:])
    power_map = (real_part * real_part + imag_part * imag_part) / float(rows_y * cols_x)
    return power_map.reshape(count, rows_y * cols_x)


def sum_kernel(axes, x_ref, o_ref, acc, full, got, send_sem, recv_sem):
    where = {name: lax.axis_index(name) for name, _ in axes}
    steps = []
    for name, size in axes:
        bit = 1
        while bit < size:
            steps.append((name, bit))
            bit *= 2

    def partner(name, bit):
        me = where[name]
        mine = lax.rem(me // bit, 2)
        return mine, {name: me + bit * (1 - 2 * mine)}

    barrier = pltpu.get_barrier_semaphore()
    for name, bit in steps:
        _, other = partner(name, bit)
        pl.semaphore_signal(barrier, inc=1, device_id=other, device_id_type=MESH)
    pl.semaphore_wait(barrier, len(steps))

    total = x_ref.shape[0]
    rows, start, offset = total, 0, 0
    acc[...] = x_ref[...]
    plan = []
    for n, (name, bit) in enumerate(steps):
        mine, other = partner(name, bit)
        split = rows % 16 == 0
        if split:
            rows //= 2
            away = start + (1 - mine) * rows
            start = start + mine * rows
        else:
            away = start
        plan.append((other, split, start, rows, mine))
        if split:
            away = pl.multiple_of(away, 8)
        here = pl.multiple_of(start, 8)
        source = x_ref if n == 0 else acc
        copy = pltpu.make_async_remote_copy(
            src_ref=source.at[pl.ds(away, rows)],
            dst_ref=got.at[pl.ds(offset, rows)],
            send_sem=send_sem.at[n],
            recv_sem=recv_sem.at[n],
            device_id=other,
            device_id_type=MESH,
        )
        copy.start()
        copy.wait()
        acc[pl.ds(here, rows)] = acc[pl.ds(here, rows)] + got[pl.ds(offset, rows)]
        offset += rows
    last = pl.ds(pl.multiple_of(start, 8), rows)
    full[last] = acc[last]
    for n in reversed(range(len(steps))):
        other, split, start, rows, mine = plan[n]
        if not split:
            continue
        here = pl.multiple_of(start, 8)
        copy = pltpu.make_async_remote_copy(
            src_ref=full.at[pl.ds(here, rows)],
            dst_ref=full.at[pl.ds(here, rows)],
            send_sem=send_sem.at[len(steps) + n],
            recv_sem=recv_sem.at[len(steps) + n],
            device_id=other,
            device_id_type=MESH,
        )
        copy.start()
        copy.wait()
    o_ref[...] = full[...]


def reduce_cov(partial_value, sizes):
    axes = [("rep", sizes["rep"]), ("pix", sizes["pix"])]
    rows, depth, count = partial_value.shape[0], 0, 0
    for _, size in axes:
        for _ in range(size.bit_length() - 1):
            if rows % 16 == 0:
                rows //= 2
            depth += rows
            count += 1
    vmem = pl.BlockSpec(memory_space=pltpu.VMEM)
    return pl.pallas_call(
        functools.partial(sum_kernel, axes),
        out_shape=jax.ShapeDtypeStruct(partial_value.shape, jnp.float32),
        in_specs=[vmem],
        out_specs=vmem,
        scratch_shapes=[
            pltpu.VMEM(partial_value.shape, jnp.float32),
            pltpu.VMEM(partial_value.shape, jnp.float32),
            pltpu.VMEM((depth, partial_value.shape[1]), jnp.float32),
            pltpu.SemaphoreType.DMA((2 * count,)),
            pltpu.SemaphoreType.DMA((2 * count,)),
        ],
        compiler_params=pltpu.CompilerParams(collective_id=0, has_side_effects=True),
        name="cov_sum",
    )(partial_value)


def lower_blocks(size):
    return [(i, j) for i in range(size // BLOCK) for j in range(i + 1)]


def stage_sum_kernel(stages, x_ref, o_ref, acc, full, got, send_sem, recv_sem):
    where = {name: lax.axis_index(name) for name in ("pix", "rep")}
    blocks = lower_blocks(x_ref.shape[0])

    def span(i):
        return slice(i * BLOCK, (i + 1) * BLOCK)

    def partner(stage, e):
        moved = dict(where)
        for b, (name, bit) in enumerate(stage):
            if e >> b & 1:
                moved[name] = moved[name] ^ bit
        return {name: moved[name] for name in {name for name, _ in stage}}

    def place(stage):
        index = 0
        for b, (name, bit) in enumerate(stage):
            index = index + (where[name] // bit % 2) * 2**b
        return index

    barrier = pltpu.get_barrier_semaphore()
    count = 0
    for stage in stages:
        for e in range(1, 2 ** len(stage)):
            pl.semaphore_signal(barrier, inc=1, device_id=partner(stage, e), device_id_type=MESH)
            count += 1
    for n, (i, j) in enumerate(blocks):
        acc[span(n)] = x_ref[span(i), span(j)] + x_ref[span(j), span(i)].T
    pl.semaphore_wait(barrier, count)

    rows, start, offset, sem = acc.shape[0], 0, 0, 0
    plan, sends = [], []
    for stage in stages:
        members = 2 ** len(stage)
        rows //= members
        index = place(stage)
        copies = []
        for e in range(1, members):
            away = pl.multiple_of(start + (index ^ e) * rows, 8)
            copies.append(
                pltpu.make_async_remote_copy(
                    src_ref=acc.at[pl.ds(away, rows)],
                    dst_ref=got.at[pl.ds(offset + (e - 1) * rows, rows)],
                    send_sem=send_sem.at[sem],
                    recv_sem=recv_sem.at[sem],
                    device_id=partner(stage, e),
                    device_id_type=MESH,
                )
            )
            copies[-1].start()
            sem += 1
        start = start + index * rows
        here = pl.ds(pl.multiple_of(start, 8), rows)
        total = acc[here]
        for e, copy in enumerate(copies):
            copy.wait_recv()
            total = total + got[offset + e * rows : offset + (e + 1) * rows]
        acc[here] = total
        plan.append((stage, start, rows))
        sends += copies
        offset += (members - 1) * rows
    full[here] = total
    for stage, start, rows in reversed(plan):
        here = pl.ds(pl.multiple_of(start, 8), rows)
        copies = []
        for e in range(1, 2 ** len(stage)):
            copies.append(
                pltpu.make_async_remote_copy(
                    src_ref=full.at[here],
                    dst_ref=full.at[here],
                    send_sem=send_sem.at[sem],
                    recv_sem=recv_sem.at[sem],
                    device_id=partner(stage, e),
                    device_id_type=MESH,
                )
            )
            copies[-1].start()
            sem += 1
        for copy in copies:
            copy.wait_recv()
        sends += copies
    for n, (i, j) in enumerate(blocks):
        o_ref[span(i), span(j)] = full[span(n)]
        if i != j:
            o_ref[span(j), span(i)] = full[span(n)].T
    for copy in sends:
        copy.wait_send()


def stage_bits(name, size):
    return [(name, 2**b) for b in range(size.bit_length() - 1)]


def sum_both(half, sizes):
    rep, pix = stage_bits("rep", sizes["rep"]), stage_bits("pix", sizes["pix"])
    stages = [s for s in (rep[:1], rep[1:] + pix[:1], pix[1:]) if s]
    size = half.shape[0]
    rows = len(lower_blocks(size)) * BLOCK
    if rows % (8 * sizes["rep"] * sizes["pix"]):
        total = reduce_cov(half, sizes)
        return total + total.T
    count = sum(2 ** len(stage) - 1 for stage in stages)
    vmem = pl.BlockSpec(memory_space=pltpu.VMEM)
    return pl.pallas_call(
        functools.partial(stage_sum_kernel, stages),
        out_shape=jax.ShapeDtypeStruct(half.shape, jnp.float32),
        in_specs=[vmem],
        out_specs=vmem,
        scratch_shapes=[
            pltpu.VMEM((rows, BLOCK), jnp.float32),
            pltpu.VMEM((rows, BLOCK), jnp.float32),
            pltpu.VMEM((rows, BLOCK), jnp.float32),
            pltpu.SemaphoreType.DMA((2 * count,)),
            pltpu.SemaphoreType.DMA((2 * count,)),
        ],
        compiler_params=pltpu.CompilerParams(
            collective_id=0, has_side_effects=True, vmem_limit_bytes=16 * 1024 * 1024
        ),
        name="cov_sum",
    )(half)


def tree_sum(terms):
    while len(terms) > 1:
        terms = [a + b for a, b in zip(terms[::2], terms[1::2])]
    return terms[0]


def splat_inverse(d):
    d = [list(r) for r in d]
    n = len(d)
    at = lambda i, j: d[min(i, j)][max(i, j)]
    for k in range(0, n, 2):
        p, q, r = d[k][k], d[k][k + 1], d[k + 1][k + 1]
        scale = 1.0 / (p * r - q * q)
        pi, qi, ri = r * scale, -(q * scale), p * scale
        others = [i for i in range(n) if i not in (k, k + 1)]
        left = {i: (at(i, k), at(i, k + 1)) for i in others}
        new = {i: (left[i][0] * pi + left[i][1] * qi, left[i][0] * qi + left[i][1] * ri) for i in others}
        for i in others:
            for j in others:
                if j >= i:
                    d[i][j] = d[i][j] - (new[i][0] * left[j][0] + new[i][1] * left[j][1])
        for i in others:
            for s in range(2):
                d[min(i, k + s)][max(i, k + s)] = new[i][s]
        d[k][k], d[k][k + 1], d[k + 1][k + 1] = -pi, -qi, -ri
    return d


def block_inverse(a, splat=splat_inverse):
    size = a.shape[0]
    shape = (8, size)
    lane = lax.broadcasted_iota(jnp.int32, shape, 1)
    sub = lax.broadcasted_iota(jnp.int32, shape, 0)
    rows = [a[8 * r : 8 * r + 8, :] for r in range(size // 8)]
    wide = lambda x: jnp.broadcast_to(x, shape)
    for t in range(size // 8):
        own = rows[t]
        cols = [wide(own[:, 8 * t + j : 8 * t + j + 1]) for j in range(8)]
        block = [[wide(cols[j][i : i + 1, :]) if j >= i else None for j in range(8)] for i in range(8)]
        minus = splat(block)
        inside = jnp.logical_and(lane >= 8 * t, lane < 8 * t + 8)
        fixed = jnp.where(inside, (lane - 8 * t == sub).astype(jnp.float32), own)
        base = [wide(fixed[s : s + 1, :]) for s in range(8)]
        new = [tree_sum([minus[min(s, m)][max(s, m)] * base[m] for m in range(8)]) for s in range(8)]
        for r in range(size // 8):
            if r == t:
                out = new[0]
                for s in range(1, 8):
                    out = jnp.where(sub == s, new[s], out)
                rows[r] = -out
            else:
                old = rows[r]
                terms = [wide(old[:, 8 * t + s : 8 * t + s + 1]) * new[s] for s in range(8)]
                rows[r] = jnp.where(inside, 0.0, old) + tree_sum(terms)
    return jnp.concatenate(rows, axis=0)

def solve_kernel(scale, cov_ref, noise_ref, table_ref, o_ref, a_ref):
    size = cov_ref.shape[0]
    blocks = size // BLOCK
    dot = functools.partial(lax.dot_general, precision=HI, preferred_element_type=jnp.float32)

    def mul(x, y):
        return dot(x, y, (((1,), (0,)), ((), ())))

    def mul_t(x, y):
        return dot(x, y, (((1,), (1,)), ((), ())))

    def span(i, j=None):
        return slice(i * BLOCK, (i + 1 if j is None else j) * BLOCK)

    a_ref[...] = cov_ref[...] * scale + noise_ref[...]
    for k in range(blocks):
        inverse = block_inverse(a_ref[span(k), span(k)])
        if k == 0:
            o_ref[...] = mul(table_ref[...], noise_ref[...])
        others = [i % blocks for i in range(k + 1, k + blocks)]
        if k + 1 < blocks:
            panel = mul(inverse, a_ref[span(k), span(k + 1, blocks)])
            for i in others:
                rest = span(k + 1, blocks)
                a_ref[span(i), rest] = a_ref[span(i), rest] - mul(a_ref[span(i), span(k)], panel)
            a_ref[span(k), span(k + 1, blocks)] = panel
        right = mul(o_ref[:, span(k)], inverse)
        for i in others:
            o_ref[:, span(i)] = o_ref[:, span(i)] - mul_t(right, a_ref[span(i), span(k)])
        o_ref[:, span(k)] = right


def filter_rows(data_cov, scale, noise_cov, table):
    vmem = pl.BlockSpec(memory_space=pltpu.VMEM)
    return pl.pallas_call(
        functools.partial(solve_kernel, scale),
        out_shape=jax.ShapeDtypeStruct(data_cov.shape, jnp.float32),
        in_specs=[vmem] * 3,
        out_specs=vmem,
        scratch_shapes=[pltpu.VMEM(data_cov.shape, jnp.float32)],
        compiler_params=pltpu.CompilerParams(vmem_limit_bytes=SMALL_LIMIT),
        name="filter_solve",
    )(data_cov, noise_cov, table)


def split(x):
    high = x.astype(jnp.bfloat16)
    return high, (x - high.astype(jnp.float32)).astype(jnp.bfloat16)


def dot3(left, right):
    (lh, ll), (rh, rl) = left, right
    one = functools.partial(jnp.dot, preferred_element_type=jnp.float32)
    return one(lh, rh) + (one(lh, rl) + one(ll, rh))


def split_table(values):
    high = values.astype(ml_dtypes.bfloat16)
    low = (values - high.astype(np.float64)).astype(ml_dtypes.bfloat16)
    return jnp.asarray(high), jnp.asarray(low)


def packed_x(length):
    idx = np.arange(length)
    half = length // 2
    phase = lambda freq: (idx[:, None] * freq[None, :] % length) * (2.0 * math.pi / length)
    cosines = np.cos(phase(np.arange(half + 1)))
    sines = np.sin(phase(np.arange(1, half)))
    return np.concatenate([cosines, sines], axis=1)


def full_y(length):
    idx = np.arange(length)
    phase = (idx[:, None] * idx[None, :] % length) * (2.0 * math.pi / length)
    return np.concatenate([np.cos(phase), np.sin(phase)], axis=0)


def cov_kernel(sky_ref, mask_ref, o_ref):
    mid = sky_ref.shape[0] // 2
    width = sky_ref.shape[1]
    step = math.gcd(width, COV_STEP)

    def dot(x, y):
        return lax.dot_general(x, y, (((1,), (1,)), ((), ())), preferred_element_type=jnp.float32)

    @pl.when(pl.program_id(0) == 0)
    def _():
        o_ref[...] = jnp.zeros_like(o_ref)

    for start in range(0, width, step):
        at = slice(start, start + step)
        high, low = split(sky_ref[:, at] * mask_ref[:, at].astype(jnp.float32))
        top, end = high[:mid], high[mid:]
        cross = dot(high, low)
        o_ref[:mid, :mid] = o_ref[:mid, :mid] + (cross[:mid, :mid] + dot(top * 0.5, top))
        o_ref[:mid, mid:] = o_ref[:mid, mid:] + cross[:mid, mid:]
        o_ref[mid:, :mid] = o_ref[mid:, :mid] + (cross[mid:, :mid] + dot(end, top))
        o_ref[mid:, mid:] = o_ref[mid:, mid:] + (cross[mid:, mid:] + dot(end * 0.5, end))


def half_covariance(sky, mask):
    channels, pixels = sky.shape
    width = math.gcd(pixels, COV_PIXELS)
    return pl.pallas_call(
        cov_kernel,
        grid=(pixels // width,),
        out_shape=jax.ShapeDtypeStruct((channels, channels), jnp.float32),
        in_specs=[
            pl.BlockSpec((channels, width), lambda i: (0, i)),
            pl.BlockSpec((1, width), lambda i: (0, i)),
        ],
        out_specs=pl.BlockSpec((channels, channels), lambda i: (0, 0)),
        compiler_params=pltpu.CompilerParams(vmem_limit_bytes=VMEM_LIMIT),
        name="covariance",
    )(sky, mask)


def spread_kernel(
    n, sky_ref, first_ref, second_ref, mask_ref, mix_ref, dxh_ref, dxl_ref, dyh_ref, dyl_ref, q_ref,
    stage, high, low, out, z, maps, load_sem, send_sem, recv_sem, own_sem, put_sem,
):
    me = lax.axis_index("pix")
    entries, _, width = high.shape
    parts = (first_ref, second_ref)
    shared = len(parts)
    rows = entries - shared
    plain = rows - shared
    chunks, turns = z.shape[0], out.shape[0]
    slots = stage.shape[0]
    group = max(d for d in range(1, GROUP + 1) if plain % d == 0)
    side = n // 2
    step = n * 8
    tall = 8 * width // LANES
    length = n * rows
    moved_rows = length - entries

    barrier = pltpu.get_barrier_semaphore()
    for k in range(1, n):
        pl.semaphore_signal(barrier, inc=1, device_id={"pix": me ^ k}, device_id_type=MESH)

    def load(ref, y, i):
        cols = pl.ds(pl.multiple_of(y * width, width), width)
        slot = lax.rem(i, slots)
        return pltpu.make_async_copy(ref.at[:, cols], stage.at[slot], load_sem.at[slot])

    def load_next(i):
        @pl.when(i < rows)
        def _():
            load(sky_ref, lax.rem(i + shared, rows), i).start()

        for e, ref in enumerate(parts):

            @pl.when(i == rows + e)
            def _():
                load(ref, 0, i).start()

    for i in range(slots):
        load(sky_ref, i + shared, i).start()
    pl.semaphore_wait(barrier, n - 1)

    def own_arrived(c):
        own = z.at[c, pl.ds(0, entries * tall)]
        pltpu.make_async_copy(own, own, own_sem.at[c]).wait()

    def others_sent(c):
        others = z.at[c, pl.ds(0, moved_rows * tall)]
        pltpu.make_async_copy(others, others, send_sem.at[c]).wait()

    def chunk(c, _):
        slot = lax.rem(c, turns)

        @pl.when(c >= turns)
        def _():
            own_arrived(c - turns)
            others_sent(c - turns)

        mix = split(mix_ref[pl.ds(pl.multiple_of(c * step, step), step), :])
        dx = (dxh_ref[...], dxl_ref[...])

        def entry(i, _):
            @pl.when(c == 0)
            def _():
                load(sky_ref, 0, i).wait()
                h, l = split(stage[lax.rem(i, slots)])
                high[i] = h
                low[i] = l
                load_next(i + slots)

            live = mask_ref[lax.rem(i + shared, rows)].astype(jnp.float32)
            field = dot3(mix, (high[i], low[i])) * jnp.where(i < rows, live, 1.0)
            moved = dot3(split(field), dx)
            for p in range(n):
                for h in range(width // LANES):
                    at = pl.ds(pl.multiple_of(i * tall + h * 8, 8), 8)
                    out[slot, p, at, :] = moved[p * 8 : (p + 1) * 8, h * LANES : (h + 1) * LANES]
            return 0

        def send(i, y, size, partners):
            here = pl.ds(pl.multiple_of(i * tall, tall), size * tall)
            there = pl.ds(pl.multiple_of(y * tall, tall), size * tall)
            for k in range(1, partners):
                pltpu.make_async_remote_copy(
                    src_ref=out.at[slot, me ^ k, here],
                    dst_ref=z.at[c, there],
                    send_sem=send_sem.at[c],
                    recv_sem=recv_sem.at[c],
                    device_id={"pix": me ^ k},
                    device_id_type=MESH,
                ).start()
            pltpu.make_async_copy(out.at[slot, me, here], z.at[c, there], own_sem.at[c]).start()

        def part(g, _):
            lax.fori_loop(g * group, (g + 1) * group, entry, 0)
            send(g * group, me * rows + shared + g * group, group, n)
            return 0

        lax.fori_loop(0, plain // group, part, 0)
        if shared:
            lax.fori_loop(plain, entries, entry, 0)
            send(plain, me * rows, shared, side)
            send(rows, (me ^ side) * rows, shared, side)
        return 0

    lax.fori_loop(0, chunks, chunk, 0)
    for c in range(chunks - turns, chunks):
        own_arrived(c)

    dy = (dyh_ref[...], dyl_ref[...])
    half = width // 2
    lane = lax.broadcasted_iota(jnp.int32, (length, half), 1)
    row_id = lax.broadcasted_iota(jnp.int32, (length, half), 0)
    first = lane == 0
    late = jnp.logical_and(first, row_id > length // 2)

    def put(c):
        slot = lax.rem(c, 2)
        return pltpu.make_async_copy(maps.at[slot], q_ref.at[c], put_sem.at[slot])

    def finish(c, _):
        others = z.at[c, pl.ds(0, moved_rows * tall)]
        pltpu.make_async_copy(others, others, recv_sem.at[c]).wait()
        slot = lax.rem(c, 2)

        @pl.when(c >= 2)
        def _():
            put(c - 2).wait()

        for j in range(8):
            field = [z[c, pl.ds(h * 8 + j, length, stride=16), :] for h in range(2)]
            both = dot3(dy, split(jnp.concatenate(field, axis=1)))
            cc, cs = both[:length, :half], both[:length, half:]
            sc, ss = both[length:, :half], both[length:, half:]
            real = jnp.where(late, cs, cc - jnp.where(first, 0.0, ss))
            imag = jnp.where(late, ss, sc + jnp.where(first, 0.0, cs))
            maps[slot, pl.ds(j, length, stride=8), :] = real * real + imag * imag
            for e, u in enumerate((0, length // 2)):
                edge = cs[u : u + 1] * cs[u : u + 1] + ss[u : u + 1] * ss[u : u + 1]
                maps[slot, pl.ds((length + e) * 8 + j, 1), :] = edge
        put(c).start()
        return 0

    lax.fori_loop(0, chunks, finish, 0)
    for c in range(max(0, chunks - 2), chunks):
        put(c).wait()

    for c in range(chunks - turns, chunks):
        others_sent(c)


def spread(sky, extras, mask, mix, n):
    channels, pixels = sky.shape
    rows = pixels // SX
    entries = rows + len(extras)
    tall = 8 * SX // LANES
    chunks = mix.shape[0] // (8 * n)
    dxh, dxl = split_table(packed_x(SX))
    dyh, dyl = split_table(full_y(n * rows) / 256.0)
    vmem = pl.BlockSpec(memory_space=pltpu.VMEM)
    hbm = pl.BlockSpec(memory_space=pl.ANY)
    return pl.pallas_call(
        functools.partial(spread_kernel, n),
        out_shape=jax.ShapeDtypeStruct((chunks, (n * rows + 2) * 8, LANES), jnp.float32),
        in_specs=[hbm] * (1 + len(extras)) + [vmem] * 6,
        out_specs=hbm,
        scratch_shapes=[
            pltpu.VMEM((4, channels, SX), jnp.float32),
            pltpu.VMEM((entries, channels, SX), jnp.bfloat16),
            pltpu.VMEM((entries, channels, SX), jnp.bfloat16),
            pltpu.VMEM((min(chunks, TURNS), n, entries * tall, LANES), jnp.float32),
            pltpu.VMEM((chunks, n * rows * tall, LANES), jnp.float32),
            pltpu.VMEM((2, (n * rows + 2) * 8, LANES), jnp.float32),
            pltpu.SemaphoreType.DMA((4,)),
            pltpu.SemaphoreType.DMA((chunks,)),
            pltpu.SemaphoreType.DMA((chunks,)),
            pltpu.SemaphoreType.DMA((chunks,)),
            pltpu.SemaphoreType.DMA((2,)),
        ],
        compiler_params=pltpu.CompilerParams(
            collective_id=1, has_side_effects=True, vmem_limit_bytes=VMEM_LIMIT
        ),
        name="spread",
    )(sky, *extras, mask.reshape(rows, 1, SX), mix, dxh, dxl, dyh, dyl)


def unfold_kernel(q_ref, o_ref):
    length = q_ref.shape[1] // 8 - 2
    shape = (8, LANES)
    lane = lax.broadcasted_iota(jnp.int32, shape, 1)
    first = lane == 0
    mirror = jnp.where(first, 0, LANES - lane)

    def tile(u):
        return q_ref[0, u * 8 : u * 8 + 8, :]

    def back(x):
        return jnp.take_along_axis(x, mirror, axis=1)

    def write(u, near, far):
        o_ref[:, u * SX : u * SX + LANES] = near
        o_ref[:, u * SX + LANES : (u + 1) * SX] = far

    for e, u in enumerate((0, length // 2)):
        a = tile(u)
        write(u, a, jnp.where(first, tile(length + e), back(a)))
    for u in range(1, length // 2):
        v = length - u
        a, b = tile(u), tile(v)
        write(u, a, back(b))
        write(v, jnp.where(first, a, b), jnp.where(first, b, back(a)))


def unfold(q):
    chunks, tall, _ = q.shape
    length = tall // 8 - 2
    return pl.pallas_call(
        unfold_kernel,
        grid=(chunks,),
        out_shape=jax.ShapeDtypeStruct((chunks * 8, length * SX), jnp.float32),
        in_specs=[pl.BlockSpec((1, tall, LANES), lambda c: (c, 0, 0))],
        out_specs=pl.BlockSpec((8, length * SX), lambda c: (c, 0)),
        compiler_params=pltpu.CompilerParams(vmem_limit_bytes=SMALL_LIMIT),
        name="unfold",
    )(q)


def local(sizes, sky_cube, pixel_mask, noise_cov):
    live = pixel_mask[0].astype(jnp.float32)
    masked = sky_cube[0] * live[None, :]
    owners = sizes["pix"]
    share = F // owners
    kernels = share % 8 == 0 and owners & (owners - 1) == 0 and masked.shape[1] % SX == 0 and SX == 2 * LANES
    table = los_table(F)
    if kernels:
        table = table.reshape(owners, share // 8, 8, F).transpose(1, 0, 2, 3).reshape(F, F)
    table = jnp.asarray(table)
    count_all = sizes["pix"] * sizes["rep"] * masked.shape[1]
    if not kernels:
        data_cov = sum_both(half_covariance(sky_cube[0], pixel_mask), sizes)
        folded = filter_rows(data_cov, 1.0 / count_all, noise_cov, table)
    else:
        across = [(p, p ^ (owners // 2)) for p in range(owners)]
        near = sky_cube[0, :, : 2 * SX] * pixel_mask[0, : 2 * SX].astype(jnp.float32)
        near, mask = lax.optimization_barrier((near, pixel_mask))
        first = lax.ppermute(near[:, :SX], "pix", across)
        data_cov = sum_both(half_covariance(sky_cube[0], mask), sizes)
        data_cov, later = lax.optimization_barrier((data_cov, near[:, SX:]))
        second = lax.ppermute(later, "pix", across)
        folded = filter_rows(data_cov, 1.0 / count_all, noise_cov, table)
        return unfold(spread(sky_cube[0], [first, second], pixel_mask, folded, owners))[None]
    eighth = share // 8
    widths = [eighth, 2 * eighth, 2 * eighth, 2 * eighth, eighth] if eighth else [share]
    by_owner = folded.reshape(owners, share, F)
    result, planes = None, []

    def place(done, at, result):
        power = sky_power(planes[done][0], SY, SX)
        if result is None:
            return jnp.pad(power, ((at, share - at - power.shape[0]), (0, 0)))
        return lax.dynamic_update_slice(result, power, (at, 0))

    starts = [sum(widths[:c]) for c in range(len(widths))]
    for c, width in enumerate(widths):
        rows = by_owner[:, starts[c] : starts[c] + width].reshape(owners * width, F)
        spectra = jnp.dot(rows, masked, precision=MID)
        stacked = spectra.reshape(owners, width, spectra.shape[1])
        if c >= 2:
            result = place(c - 2, starts[c - 2], result)
            stacked, result = lax.optimization_barrier((stacked, result))
        planes.append(lax.all_to_all(stacked, "pix", split_axis=0, concat_axis=2, tiled=True))
    for done in range(max(0, len(widths) - 2), len(widths)):
        result = place(done, starts[done], result)
    return result[None]


def solution(mesh):
    placed = (P("rep", None, "pix"), P("rep", "pix"), P())
    return jax.shard_map(
        functools.partial(local, dict(mesh.shape)),
        mesh=mesh,
        in_specs=placed,
        out_specs=P("rep", "pix", None),
        check_vma=False,
    )
```

```python
import functools
import math

import jax
import jax.numpy as jnp
import ml_dtypes
import numpy as np
from jax import lax
from jax.experimental import pallas as pl
from jax.experimental.pallas import tpu as pltpu
from jax.sharding import PartitionSpec as P

F = 512
SY = 256
SX = 256
BLOCK = 128
GROUP = 3
TURNS = 4
COV_PIXELS = 2048
COV_STEP = 256
LANES = 128
VMEM_LIMIT = 52 * 1024 * 1024
SMALL_LIMIT = 24 * 1024 * 1024

HI = lax.Precision.HIGHEST
MID = lax.Precision.HIGH
MESH = pl.DeviceIdType.MESH


def dft_pair(length):
    idx = jnp.arange(length, dtype=jnp.int32)
    phase = (idx[:, None] * idx[None, :] % length).astype(jnp.float32) * (2.0 * math.pi / length)
    return (jnp.cos(phase), jnp.sin(phase))


def los_table(length):
    idx = np.arange(length)
    half_len = length // 2
    freq = np.where(idx <= half_len, idx, idx - half_len)
    phase = (freq[:, None] * idx[None, :] % length) * (2.0 * math.pi / length)
    values = np.where((idx <= half_len)[:, None], np.cos(phase), np.sin(phase))
    edge = np.logical_or(idx == 0, idx == half_len)
    scale = np.where(edge, math.sqrt(1.0 / length), math.sqrt(2.0 / length))
    return (values * scale[:, None]).astype(np.float32)


def sky_power(planes, rows_y, cols_x):
    count = planes.shape[0]
    field = planes.reshape(count, rows_y, cols_x)
    cos_x, sin_x = dft_pair(cols_x)
    cos_y, sin_y = dft_pair(rows_y)
    both_x = jnp.concatenate([cos_x, sin_x], axis=1)
    both_y = jnp.concatenate([cos_y, sin_y], axis=0)
    first = jnp.einsum("kyx,xw->kyw", field, both_x, precision=MID)
    second = jnp.einsum("vy,kyw->kvw", both_y, first, precision=MID)
    real_part = second[:, :rows_y, :cols_x] - second[:, rows_y:, cols_x:]
    imag_part = -(second[:, rows_y:, :cols_x] + second[:, :rows_y, cols_x:])
    power_map = (real_part * real_part + imag_part * imag_part) / float(rows_y * cols_x)
    return power_map.reshape(count, rows_y * cols_x)


def sum_kernel(axes, x_ref, o_ref, acc, full, got, send_sem, recv_sem):
    where = {name: lax.axis_index(name) for name, _ in axes}
    steps = []
    for name, size in axes:
        bit = 1
        while bit < size:
            steps.append((name, bit))
            bit *= 2

    def partner(name, bit):
        me = where[name]
        mine = lax.rem(me // bit, 2)
        return mine, {name: me + bit * (1 - 2 * mine)}

    barrier = pltpu.get_barrier_semaphore()
    for name, bit in steps:
        _, other = partner(name, bit)
        pl.semaphore_signal(barrier, inc=1, device_id=other, device_id_type=MESH)
    pl.semaphore_wait(barrier, len(steps))

    total = x_ref.shape[0]
    rows, start, offset = total, 0, 0
    acc[...] = x_ref[...]
    plan = []
    for n, (name, bit) in enumerate(steps):
        mine, other = partner(name, bit)
        split = rows % 16 == 0
        if split:
            rows //= 2
            away = start + (1 - mine) * rows
            start = start + mine * rows
        else:
            away = start
        plan.append((other, split, start, rows, mine))
        if split:
            away = pl.multiple_of(away, 8)
        here = pl.multiple_of(start, 8)
        source = x_ref if n == 0 else acc
        copy = pltpu.make_async_remote_copy(
            src_ref=source.at[pl.ds(away, rows)],
            dst_ref=got.at[pl.ds(offset, rows)],
            send_sem=send_sem.at[n],
            recv_sem=recv_sem.at[n],
            device_id=other,
            device_id_type=MESH,
        )
        copy.start()
        copy.wait()
        acc[pl.ds(here, rows)] = acc[pl.ds(here, rows)] + got[pl.ds(offset, rows)]
        offset += rows
    last = pl.ds(pl.multiple_of(start, 8), rows)
    full[last] = acc[last]
    for n in reversed(range(len(steps))):
        other, split, start, rows, mine = plan[n]
        if not split:
            continue
        here = pl.multiple_of(start, 8)
        copy = pltpu.make_async_remote_copy(
            src_ref=full.at[pl.ds(here, rows)],
            dst_ref=full.at[pl.ds(here, rows)],
            send_sem=send_sem.at[len(steps) + n],
            recv_sem=recv_sem.at[len(steps) + n],
            device_id=other,
            device_id_type=MESH,
        )
        copy.start()
        copy.wait()
    o_ref[...] = full[...]


def reduce_cov(partial_value, sizes):
    axes = [("rep", sizes["rep"]), ("pix", sizes["pix"])]
    rows, depth, count = partial_value.shape[0], 0, 0
    for _, size in axes:
        for _ in range(size.bit_length() - 1):
            if rows % 16 == 0:
                rows //= 2
            depth += rows
            count += 1
    vmem = pl.BlockSpec(memory_space=pltpu.VMEM)
    return pl.pallas_call(
        functools.partial(sum_kernel, axes),
        out_shape=jax.ShapeDtypeStruct(partial_value.shape, jnp.float32),
        in_specs=[vmem],
        out_specs=vmem,
        scratch_shapes=[
            pltpu.VMEM(partial_value.shape, jnp.float32),
            pltpu.VMEM(partial_value.shape, jnp.float32),
            pltpu.VMEM((depth, partial_value.shape[1]), jnp.float32),
            pltpu.SemaphoreType.DMA((2 * count,)),
            pltpu.SemaphoreType.DMA((2 * count,)),
        ],
        compiler_params=pltpu.CompilerParams(collective_id=0, has_side_effects=True),
        name="cov_sum",
    )(partial_value)


def lower_blocks(size):
    return [(i, j) for i in range(size // BLOCK) for j in range(i + 1)]


def stage_sum_kernel(stages, x_ref, o_ref, acc, full, got, send_sem, recv_sem):
    where = {name: lax.axis_index(name) for name in ("pix", "rep")}
    blocks = lower_blocks(x_ref.shape[0])

    def span(i):
        return slice(i * BLOCK, (i + 1) * BLOCK)

    def partner(stage, e):
        moved = dict(where)
        for b, (name, bit) in enumerate(stage):
            if e >> b & 1:
                moved[name] = moved[name] ^ bit
        return {name: moved[name] for name in {name for name, _ in stage}}

    def place(stage):
        index = 0
        for b, (name, bit) in enumerate(stage):
            index = index + (where[name] // bit % 2) * 2**b
        return index

    barrier = pltpu.get_barrier_semaphore()
    count = 0
    for stage in stages:
        for e in range(1, 2 ** len(stage)):
            pl.semaphore_signal(barrier, inc=1, device_id=partner(stage, e), device_id_type=MESH)
            count += 1
    for n, (i, j) in enumerate(blocks):
        acc[span(n)] = x_ref[span(i), span(j)] + x_ref[span(j), span(i)].T
    pl.semaphore_wait(barrier, count)

    rows, start, offset, sem = acc.shape[0], 0, 0, 0
    plan, sends = [], []
    for stage in stages:
        members = 2 ** len(stage)
        rows //= members
        index = place(stage)
        copies = []
        for e in range(1, members):
            away = pl.multiple_of(start + (index ^ e) * rows, 8)
            copies.append(
                pltpu.make_async_remote_copy(
                    src_ref=acc.at[pl.ds(away, rows)],
                    dst_ref=got.at[pl.ds(offset + (e - 1) * rows, rows)],
                    send_sem=send_sem.at[sem],
                    recv_sem=recv_sem.at[sem],
                    device_id=partner(stage, e),
                    device_id_type=MESH,
                )
            )
            copies[-1].start()
            sem += 1
        start = start + index * rows
        here = pl.ds(pl.multiple_of(start, 8), rows)
        total = acc[here]
        for e, copy in enumerate(copies):
            copy.wait_recv()
            total = total + got[offset + e * rows : offset + (e + 1) * rows]
        acc[here] = total
        plan.append((stage, start, rows))
        sends += copies
        offset += (members - 1) * rows
    full[here] = total
    for stage, start, rows in reversed(plan):
        here = pl.ds(pl.multiple_of(start, 8), rows)
        copies = []
        for e in range(1, 2 ** len(stage)):
            copies.append(
                pltpu.make_async_remote_copy(
                    src_ref=full.at[here],
                    dst_ref=full.at[here],
                    send_sem=send_sem.at[sem],
                    recv_sem=recv_sem.at[sem],
                    device_id=partner(stage, e),
                    device_id_type=MESH,
                )
            )
            copies[-1].start()
            sem += 1
        for copy in copies:
            copy.wait_recv()
        sends += copies
    for n, (i, j) in enumerate(blocks):
        o_ref[span(i), span(j)] = full[span(n)]
        if i != j:
            o_ref[span(j), span(i)] = full[span(n)].T
    for copy in sends:
        copy.wait_send()


def stage_bits(name, size):
    return [(name, 2**b) for b in range(size.bit_length() - 1)]


def sum_both(half, sizes):
    rep, pix = stage_bits("rep", sizes["rep"]), stage_bits("pix", sizes["pix"])
    stages = [s for s in (rep[:1], rep[1:] + pix[:1], pix[1:]) if s]
    size = half.shape[0]
    rows = len(lower_blocks(size)) * BLOCK
    if rows % (8 * sizes["rep"] * sizes["pix"]):
        total = reduce_cov(half, sizes)
        return total + total.T
    count = sum(2 ** len(stage) - 1 for stage in stages)
    vmem = pl.BlockSpec(memory_space=pltpu.VMEM)
    return pl.pallas_call(
        functools.partial(stage_sum_kernel, stages),
        out_shape=jax.ShapeDtypeStruct(half.shape, jnp.float32),
        in_specs=[vmem],
        out_specs=vmem,
        scratch_shapes=[
            pltpu.VMEM((rows, BLOCK), jnp.float32),
            pltpu.VMEM((rows, BLOCK), jnp.float32),
            pltpu.VMEM((rows, BLOCK), jnp.float32),
            pltpu.SemaphoreType.DMA((2 * count,)),
            pltpu.SemaphoreType.DMA((2 * count,)),
        ],
        compiler_params=pltpu.CompilerParams(
            collective_id=0, has_side_effects=True, vmem_limit_bytes=16 * 1024 * 1024
        ),
        name="cov_sum",
    )(half)


def tree_sum(terms):
    while len(terms) > 1:
        terms = [a + b for a, b in zip(terms[::2], terms[1::2])]
    return terms[0]


def splat_inverse(d):
    d = [list(r) for r in d]
    n = len(d)
    at = lambda i, j: d[min(i, j)][max(i, j)]
    for k in range(0, n, 2):
        p, q, r = d[k][k], d[k][k + 1], d[k + 1][k + 1]
        scale = 1.0 / (p * r - q * q)
        pi, qi, ri = r * scale, -(q * scale), p * scale
        others = [i for i in range(n) if i not in (k, k + 1)]
        left = {i: (at(i, k), at(i, k + 1)) for i in others}
        new = {i: (left[i][0] * pi + left[i][1] * qi, left[i][0] * qi + left[i][1] * ri) for i in others}
        for i in others:
            for j in others:
                if j >= i:
                    d[i][j] = d[i][j] - (new[i][0] * left[j][0] + new[i][1] * left[j][1])
        for i in others:
            for s in range(2):
                d[min(i, k + s)][max(i, k + s)] = new[i][s]
        d[k][k], d[k][k + 1], d[k + 1][k + 1] = -pi, -qi, -ri
    return d


def block_inverse(a, splat=splat_inverse):
    size = a.shape[0]
    shape = (8, size)
    lane = lax.broadcasted_iota(jnp.int32, shape, 1)
    sub = lax.broadcasted_iota(jnp.int32, shape, 0)
    rows = [a[8 * r : 8 * r + 8, :] for r in range(size // 8)]
    wide = lambda x: jnp.broadcast_to(x, shape)
    for t in range(size // 8):
        own = rows[t]
        cols = [wide(own[:, 8 * t + j : 8 * t + j + 1]) for j in range(8)]
        block = [[wide(cols[j][i : i + 1, :]) if j >= i else None for j in range(8)] for i in range(8)]
        minus = splat(block)
        inside = jnp.logical_and(lane >= 8 * t, lane < 8 * t + 8)
        fixed = jnp.where(inside, (lane - 8 * t == sub).astype(jnp.float32), own)
        base = [wide(fixed[s : s + 1, :]) for s in range(8)]
        new = [tree_sum([minus[min(s, m)][max(s, m)] * base[m] for m in range(8)]) for s in range(8)]
        for r in range(size // 8):
            if r == t:
                out = new[0]
                for s in range(1, 8):
                    out = jnp.where(sub == s, new[s], out)
                rows[r] = -out
            else:
                old = rows[r]
                terms = [wide(old[:, 8 * t + s : 8 * t + s + 1]) * new[s] for s in range(8)]
                rows[r] = jnp.where(inside, 0.0, old) + tree_sum(terms)
    return jnp.concatenate(rows, axis=0)

def solve_kernel(scale, cov_ref, noise_ref, table_ref, o_ref, a_ref):
    size = cov_ref.shape[0]
    blocks = size // BLOCK
    dot = functools.partial(lax.dot_general, precision=HI, preferred_element_type=jnp.float32)

    def mul(x, y):
        return dot(x, y, (((1,), (0,)), ((), ())))

    def mul_t(x, y):
        return dot(x, y, (((1,), (1,)), ((), ())))

    def span(i, j=None):
        return slice(i * BLOCK, (i + 1 if j is None else j) * BLOCK)

    a_ref[...] = cov_ref[...] * scale + noise_ref[...]
    for k in range(blocks):
        inverse = block_inverse(a_ref[span(k), span(k)])
        if k == 0:
            o_ref[...] = mul(table_ref[...], noise_ref[...])
        others = [i % blocks for i in range(k + 1, k + blocks)]
        if k + 1 < blocks:
            panel = mul(inverse, a_ref[span(k), span(k + 1, blocks)])
            for i in others:
                rest = span(k + 1, blocks)
                a_ref[span(i), rest] = a_ref[span(i), rest] - mul(a_ref[span(i), span(k)], panel)
            a_ref[span(k), span(k + 1, blocks)] = panel
        right = mul(o_ref[:, span(k)], inverse)
        for i in others:
            o_ref[:, span(i)] = o_ref[:, span(i)] - mul_t(right, a_ref[span(i), span(k)])
        o_ref[:, span(k)] = right


def filter_rows(data_cov, scale, noise_cov, table):
    vmem = pl.BlockSpec(memory_space=pltpu.VMEM)
    return pl.pallas_call(
        functools.partial(solve_kernel, scale),
        out_shape=jax.ShapeDtypeStruct(data_cov.shape, jnp.float32),
        in_specs=[vmem] * 3,
        out_specs=vmem,
        scratch_shapes=[pltpu.VMEM(data_cov.shape, jnp.float32)],
        compiler_params=pltpu.CompilerParams(vmem_limit_bytes=SMALL_LIMIT),
        name="filter_solve",
    )(data_cov, noise_cov, table)


def split(x):
    high = x.astype(jnp.bfloat16)
    return high, (x - high.astype(jnp.float32)).astype(jnp.bfloat16)


def dot3(left, right):
    (lh, ll), (rh, rl) = left, right
    one = functools.partial(jnp.dot, preferred_element_type=jnp.float32)
    return one(lh, rh) + (one(lh, rl) + one(ll, rh))


def split_table(values):
    high = values.astype(ml_dtypes.bfloat16)
    low = (values - high.astype(np.float64)).astype(ml_dtypes.bfloat16)
    return jnp.asarray(high), jnp.asarray(low)


def packed_x(length):
    idx = np.arange(length)
    half = length // 2
    phase = lambda freq: (idx[:, None] * freq[None, :] % length) * (2.0 * math.pi / length)
    cosines = np.cos(phase(np.arange(half + 1)))
    sines = np.sin(phase(np.arange(1, half)))
    return np.concatenate([cosines, sines], axis=1)


def full_y(length):
    idx = np.arange(length)
    phase = (idx[:, None] * idx[None, :] % length) * (2.0 * math.pi / length)
    return np.concatenate([np.cos(phase), np.sin(phase)], axis=0)


def cov_kernel(sky_ref, mask_ref, o_ref):
    mid = sky_ref.shape[0] // 2
    width = sky_ref.shape[1]
    step = math.gcd(width, COV_STEP)

    def dot(x, y):
        return lax.dot_general(x, y, (((1,), (1,)), ((), ())), preferred_element_type=jnp.float32)

    @pl.when(pl.program_id(0) == 0)
    def _():
        o_ref[...] = jnp.zeros_like(o_ref)

    for start in range(0, width, step):
        at = slice(start, start + step)
        high, low = split(sky_ref[:, at] * mask_ref[:, at].astype(jnp.float32))
        top, end = high[:mid], high[mid:]
        cross = dot(high, low)
        o_ref[:mid, :mid] = o_ref[:mid, :mid] + (cross[:mid, :mid] + dot(top * 0.5, top))
        o_ref[:mid, mid:] = o_ref[:mid, mid:] + cross[:mid, mid:]
        o_ref[mid:, :mid] = o_ref[mid:, :mid] + (cross[mid:, :mid] + dot(end, top))
        o_ref[mid:, mid:] = o_ref[mid:, mid:] + (cross[mid:, mid:] + dot(end * 0.5, end))


def half_covariance(sky, mask):
    channels, pixels = sky.shape
    width = math.gcd(pixels, COV_PIXELS)
    return pl.pallas_call(
        cov_kernel,
        grid=(pixels // width,),
        out_shape=jax.ShapeDtypeStruct((channels, channels), jnp.float32),
        in_specs=[
            pl.BlockSpec((channels, width), lambda i: (0, i)),
            pl.BlockSpec((1, width), lambda i: (0, i)),
        ],
        out_specs=pl.BlockSpec((channels, channels), lambda i: (0, 0)),
        compiler_params=pltpu.CompilerParams(vmem_limit_bytes=VMEM_LIMIT),
        name="covariance",
    )(sky, mask)


def spread_kernel(
    n, sky_ref, first_ref, second_ref, mask_ref, mix_ref, dxh_ref, dxl_ref, dyh_ref, dyl_ref, q_ref,
    stage, high, low, out, z, maps, load_sem, send_sem, recv_sem, own_sem, put_sem,
):
    me = lax.axis_index("pix")
    entries, _, width = high.shape
    parts = (first_ref, second_ref)
    shared = len(parts)
    rows = entries - shared
    plain = rows - shared
    chunks, turns = z.shape[0], out.shape[0]
    slots = stage.shape[0]
    group = max(d for d in range(1, GROUP + 1) if plain % d == 0)
    side = n // 2
    step = n * 8
    tall = 8 * width // LANES
    length = n * rows
    moved_rows = length - entries

    barrier = pltpu.get_barrier_semaphore()
    for k in range(1, n):
        pl.semaphore_signal(barrier, inc=1, device_id={"pix": me ^ k}, device_id_type=MESH)

    def load(ref, y, i):
        cols = pl.ds(pl.multiple_of(y * width, width), width)
        slot = lax.rem(i, slots)
        return pltpu.make_async_copy(ref.at[:, cols], stage.at[slot], load_sem.at[slot])

    def load_next(i):
        @pl.when(i < rows)
        def _():
            load(sky_ref, lax.rem(i + shared, rows), i).start()

        for e, ref in enumerate(parts):

            @pl.when(i == rows + e)
            def _():
                load(ref, 0, i).start()

    for i in range(slots):
        load(sky_ref, i + shared, i).start()
    pl.semaphore_wait(barrier, n - 1)

    def own_arrived(c):
        own = z.at[c, pl.ds(0, entries * tall)]
        pltpu.make_async_copy(own, own, own_sem.at[c]).wait()

    def others_sent(c):
        others = z.at[c, pl.ds(0, moved_rows * tall)]
        pltpu.make_async_copy(others, others, send_sem.at[c]).wait()

    def chunk(c, _):
        slot = lax.rem(c, turns)

        @pl.when(c >= turns)
        def _():
            own_arrived(c - turns)
            others_sent(c - turns)

        mix = split(mix_ref[pl.ds(pl.multiple_of(c * step, step), step), :])
        dx = (dxh_ref[...], dxl_ref[...])

        def entry(i, _):
            @pl.when(c == 0)
            def _():
                load(sky_ref, 0, i).wait()
                h, l = split(stage[lax.rem(i, slots)])
                high[i] = h
                low[i] = l
                load_next(i + slots)

            live = mask_ref[lax.rem(i + shared, rows)].astype(jnp.float32)
            field = dot3(mix, (high[i], low[i])) * jnp.where(i < rows, live, 1.0)
            moved = dot3(split(field), dx)
            for p in range(n):
                for h in range(width // LANES):
                    at = pl.ds(pl.multiple_of(i * tall + h * 8, 8), 8)
                    out[slot, p, at, :] = moved[p * 8 : (p + 1) * 8, h * LANES : (h + 1) * LANES]
            return 0

        def send(i, y, size, partners):
            here = pl.ds(pl.multiple_of(i * tall, tall), size * tall)
            there = pl.ds(pl.multiple_of(y * tall, tall), size * tall)
            for k in range(1, partners):
                pltpu.make_async_remote_copy(
                    src_ref=out.at[slot, me ^ k, here],
                    dst_ref=z.at[c, there],
                    send_sem=send_sem.at[c],
                    recv_sem=recv_sem.at[c],
                    device_id={"pix": me ^ k},
                    device_id_type=MESH,
                ).start()
            pltpu.make_async_copy(out.at[slot, me, here], z.at[c, there], own_sem.at[c]).start()

        def part(g, _):
            lax.fori_loop(g * group, (g + 1) * group, entry, 0)
            send(g * group, me * rows + shared + g * group, group, n)
            return 0

        lax.fori_loop(0, plain // group, part, 0)
        if shared:
            lax.fori_loop(plain, entries, entry, 0)
            send(plain, me * rows, shared, side)
            send(rows, (me ^ side) * rows, shared, side)
        return 0

    lax.fori_loop(0, chunks, chunk, 0)
    for c in range(chunks - turns, chunks):
        own_arrived(c)

    dy = (dyh_ref[...], dyl_ref[...])
    half = width // 2
    lane = lax.broadcasted_iota(jnp.int32, (length, half), 1)
    row_id = lax.broadcasted_iota(jnp.int32, (length, half), 0)
    first = lane == 0
    late = jnp.logical_and(first, row_id > length // 2)

    def put(c):
        slot = lax.rem(c, 2)
        return pltpu.make_async_copy(maps.at[slot], q_ref.at[c], put_sem.at[slot])

    def finish(c, _):
        others = z.at[c, pl.ds(0, moved_rows * tall)]
        pltpu.make_async_copy(others, others, recv_sem.at[c]).wait()
        slot = lax.rem(c, 2)

        @pl.when(c >= 2)
        def _():
            put(c - 2).wait()

        for j in range(8):
            field = [z[c, pl.ds(h * 8 + j, length, stride=16), :] for h in range(2)]
            both = dot3(dy, split(jnp.concatenate(field, axis=1)))
            cc, cs = both[:length, :half], both[:length, half:]
            sc, ss = both[length:, :half], both[length:, half:]
            real = jnp.where(late, cs, cc - jnp.where(first, 0.0, ss))
            imag = jnp.where(late, ss, sc + jnp.where(first, 0.0, cs))
            maps[slot, pl.ds(j, length, stride=8), :] = real * real + imag * imag
            for e, u in enumerate((0, length // 2)):
                edge = cs[u : u + 1] * cs[u : u + 1] + ss[u : u + 1] * ss[u : u + 1]
                maps[slot, pl.ds((length + e) * 8 + j, 1), :] = edge
        put(c).start()
        return 0

    lax.fori_loop(0, chunks, finish, 0)
    for c in range(max(0, chunks - 2), chunks):
        put(c).wait()

    for c in range(chunks - turns, chunks):
        others_sent(c)


def spread(sky, extras, mask, mix, n):
    channels, pixels = sky.shape
    rows = pixels // SX
    entries = rows + len(extras)
    tall = 8 * SX // LANES
    chunks = mix.shape[0] // (8 * n)
    dxh, dxl = split_table(packed_x(SX))
    dyh, dyl = split_table(full_y(n * rows) / 256.0)
    vmem = pl.BlockSpec(memory_space=pltpu.VMEM)
    hbm = pl.BlockSpec(memory_space=pl.ANY)
    return pl.pallas_call(
        functools.partial(spread_kernel, n),
        out_shape=jax.ShapeDtypeStruct((chunks, (n * rows + 2) * 8, LANES), jnp.float32),
        in_specs=[hbm] * (1 + len(extras)) + [vmem] * 6,
        out_specs=hbm,
        scratch_shapes=[
            pltpu.VMEM((4, channels, SX), jnp.float32),
            pltpu.VMEM((entries, channels, SX), jnp.bfloat16),
            pltpu.VMEM((entries, channels, SX), jnp.bfloat16),
            pltpu.VMEM((min(chunks, TURNS), n, entries * tall, LANES), jnp.float32),
            pltpu.VMEM((chunks, n * rows * tall, LANES), jnp.float32),
            pltpu.VMEM((2, (n * rows + 2) * 8, LANES), jnp.float32),
            pltpu.SemaphoreType.DMA((4,)),
            pltpu.SemaphoreType.DMA((chunks,)),
            pltpu.SemaphoreType.DMA((chunks,)),
            pltpu.SemaphoreType.DMA((chunks,)),
            pltpu.SemaphoreType.DMA((2,)),
        ],
        compiler_params=pltpu.CompilerParams(
            collective_id=1, has_side_effects=True, vmem_limit_bytes=VMEM_LIMIT
        ),
        name="spread",
    )(sky, *extras, mask.reshape(rows, 1, SX), mix, dxh, dxl, dyh, dyl)


def unfold_kernel(q_ref, o_ref):
    length = q_ref.shape[1] // 8 - 2
    shape = (8, LANES)
    lane = lax.broadcasted_iota(jnp.int32, shape, 1)
    first = lane == 0
    mirror = jnp.where(first, 0, LANES - lane)

    def tile(u):
        return q_ref[0, u * 8 : u * 8 + 8, :]

    def back(x):
        return jnp.take_along_axis(x, mirror, axis=1)

    def write(u, near, far):
        o_ref[:, u * SX : u * SX + LANES] = near
        o_ref[:, u * SX + LANES : (u + 1) * SX] = far

    for e, u in enumerate((0, length // 2)):
        a = tile(u)
        write(u, a, jnp.where(first, tile(length + e), back(a)))
    for u in range(1, length // 2):
        v = length - u
        a, b = tile(u), tile(v)
        write(u, a, back(b))
        write(v, jnp.where(first, a, b), jnp.where(first, b, back(a)))


def unfold(q):
    chunks, tall, _ = q.shape
    length = tall // 8 - 2
    return pl.pallas_call(
        unfold_kernel,
        grid=(chunks,),
        out_shape=jax.ShapeDtypeStruct((chunks * 8, length * SX), jnp.float32),
        in_specs=[pl.BlockSpec((1, tall, LANES), lambda c: (c, 0, 0))],
        out_specs=pl.BlockSpec((8, length * SX), lambda c: (c, 0)),
        compiler_params=pltpu.CompilerParams(vmem_limit_bytes=SMALL_LIMIT),
        name="unfold",
    )(q)


def local(sizes, sky_cube, pixel_mask, noise_cov):
    live = pixel_mask[0].astype(jnp.float32)
    masked = sky_cube[0] * live[None, :]
    owners = sizes["pix"]
    share = F // owners
    kernels = share % 8 == 0 and owners & (owners - 1) == 0 and masked.shape[1] % SX == 0 and SX == 2 * LANES
    table = los_table(F)
    if kernels:
        table = table.reshape(owners, share // 8, 8, F).transpose(1, 0, 2, 3).reshape(F, F)
    table = jnp.asarray(table)
    count_all = sizes["pix"] * sizes["rep"] * masked.shape[1]
    if not kernels:
        data_cov = sum_both(half_covariance(sky_cube[0], pixel_mask), sizes)
        folded = filter_rows(data_cov, 1.0 / count_all, noise_cov, table)
    else:
        across = [(p, p ^ (owners // 2)) for p in range(owners)]
        near = sky_cube[0, :, : 2 * SX] * pixel_mask[0, : 2 * SX].astype(jnp.float32)
        near, mask = lax.optimization_barrier((near, pixel_mask))
        first = lax.ppermute(near[:, :SX], "pix", across)
        data_cov = sum_both(half_covariance(sky_cube[0], mask), sizes)
        data_cov, later = lax.optimization_barrier((data_cov, near[:, SX:]))
        second = lax.ppermute(later, "pix", across)
        folded = filter_rows(data_cov, 1.0 / count_all, noise_cov, table)
        return unfold(spread(sky_cube[0], [first, second], pixel_mask, folded, owners))[None]
    eighth = share // 8
    widths = [eighth, 2 * eighth, 2 * eighth, 2 * eighth, eighth] if eighth else [share]
    by_owner = folded.reshape(owners, share, F)
    result, planes = None, []

    def place(done, at, result):
        power = sky_power(planes[done][0], SY, SX)
        if result is None:
            return jnp.pad(power, ((at, share - at - power.shape[0]), (0, 0)))
        return lax.dynamic_update_slice(result, power, (at, 0))

    starts = [sum(widths[:c]) for c in range(len(widths))]
    for c, width in enumerate(widths):
        rows = by_owner[:, starts[c] : starts[c] + width].reshape(owners * width, F)
        spectra = jnp.dot(rows, masked, precision=MID)
        stacked = spectra.reshape(owners, width, spectra.shape[1])
        if c >= 2:
            result = place(c - 2, starts[c - 2], result)
            stacked, result = lax.optimization_barrier((stacked, result))
        planes.append(lax.all_to_all(stacked, "pix", split_axis=0, concat_axis=2, tiled=True))
    for done in range(max(0, len(widths) - 2), len(widths)):
        result = place(done, starts[done], result)
    return result[None]


def solution(mesh):
    placed = (P("rep", None, "pix"), P("rep", "pix"), P())
    return jax.shard_map(
        functools.partial(local, dict(mesh.shape)),
        mesh=mesh,
        in_specs=placed,
        out_specs=P("rep", "pix", None),
        check_vma=False,
    )
```
